32 devices in a mesh: dp: 8 (over z, x), ctx: 4 (over y, core).
Axes of the slice: x: 2, y: 2, z: 4, core: 2. Of those that a mesh axis runs over, the one named last changes fastest.
Arguments:
- q_short: bfloat16 [6144, 1024], P('dp', 'ctx'), may hold values from -64 to 64
- k_short: bfloat16 [6144, 1024], P('dp', 'ctx'), may hold values from -8 to 8
- v_short: bfloat16 [6144, 1024], P('dp', 'ctx'), may hold values from -6 to 6
- dout_short: bfloat16 [6144, 1024], P('dp', 'ctx'), may hold values from -6 to 6
- doc_lengths: int32 [8, 8], replicated, may hold values from 1 to 256, as said below
- doc_dest: int32 [8, 8], replicated, may hold values from 0 to 7, as said below
- q_long: bfloat16 [8, 512, 1024], P('dp', 'ctx'), may hold values from -64 to 64
- k_long: bfloat16 [8, 512, 1024], P('dp', 'ctx'), may hold values from -8 to 8
- v_long: bfloat16 [8, 512, 1024], P('dp', 'ctx'), may hold values from -6 to 6
- dout_long: bfloat16 [8, 512, 1024], P('dp', 'ctx'), may hold values from -6 to 6
- block_order: int32 [8], replicated, may hold values from 0 to 7, each once
Outputs:
- out_short: bfloat16 [7168, 1024], P('dp', 'ctx')
- dq_short: bfloat16 [6144, 1024], P('dp', 'ctx')
- dk_short: bfloat16 [6144, 1024], P('dp', 'ctx')
- dv_short: bfloat16 [6144, 1024], P('dp', 'ctx')
- out_long: bfloat16 [8, 512, 1024], P('dp', 'ctx')
- dq_long: bfloat16 [8, 512, 1024], P('dp', 'ctx')
- dk_long: bfloat16 [8, 512, 1024], P('dp', 'ctx')
- dv_long: bfloat16 [8, 512, 1024], P('dp', 'ctx')
The draws below stay inside these ranges and needn't reach their ends.
Inputs may be any that keep to these rules, and one draw needn't show every extreme that they name: `doc_lengths`: row r lists in order the lengths of the documents packed on rank r; each row sums to 768. `doc_dest`: entry [r, j] is r, except that in each pair of ranks r and r + 4 exactly one assigns its last document to the other; such a document has at most 128 tokens, and some has exactly 128. `block_order`: A permutation.
All inputs are finite; a program needn't handle non-finite values.
Results may differ from the reference program's by a relative error of at most 0.015.
Values may be sent and summed in bfloat16 or wider, within the bound.
No kernel may reach another device: no remote copies, remote signals or barrier semaphores. Data moves between devices by JAX's collectives and lax.ppermute only.
A program may use at most 64 MiB of HBM per device.

```python
import jax
import jax.numpy as jnp
from jax import lax

HEAD_DIM = 128
HF = 1024
SHORT_DEV = 768
DOCS = 8
CAP = 256
MOVE = 128
LONG_DEV = 128
LONG = 512
N_DP = 8
N_CTX = 4


def joint_draw(key, shape):
    key_q = jax.random.fold_in(key, 101)
    key_k = jax.random.fold_in(key, 102)
    queries = jnp.clip(jax.random.normal(key_q, shape, jnp.float32), -6.0, 6.0)
    keys_out = jnp.clip(jax.random.normal(key_k, shape, jnp.float32), -6.0, 6.0)
    return (queries, keys_out)


def plan_draw(key):
    half = N_DP // 2
    ranks = jnp.arange(N_DP, dtype=jnp.int32)
    flips = jax.random.randint(jax.random.fold_in(key, 201), (half,), 0, 2)
    heavy = jnp.concatenate([flips, 1 - flips]) == 1
    chosen = jax.random.randint(jax.random.fold_in(key, 202), (), 0, half)
    tails = jax.random.randint(jax.random.fold_in(key, 203), (N_DP,), MOVE // 2, MOVE + 1)
    tails = jnp.where(ranks % half == chosen, MOVE, tails)
    big_slot = jax.random.randint(jax.random.fold_in(key, 204), (N_DP,), 0, DOCS - 1)
    shares = jax.random.randint(jax.random.fold_in(key, 205), (N_DP, DOCS), 1, 5)
    slots = jnp.arange(DOCS, dtype=jnp.int32)[None, :]
    low_heavy = SHORT_DEV // 96
    others = (slots != DOCS - 1) & (slots != big_slot[:, None])
    share_sum = jnp.sum(jnp.where(others, shares, 0), axis=1)
    spare = SHORT_DEV - CAP - tails - (DOCS - 2) * low_heavy
    extra = jnp.where(others, spare[:, None] * shares // share_sum[:, None], 0)
    leftover = spare - jnp.sum(extra, axis=1)
    first_other = jnp.where(big_slot == 0, 1, 0)
    extra = extra + jnp.where(slots == first_other[:, None], leftover[:, None], 0)
    heavy_row = jnp.where(others, low_heavy + extra, 0) + jnp.where(slots == big_slot[:, None], CAP, 0) + jnp.where(slots == DOCS - 1, tails[:, None], 0)
    low_light = SHORT_DEV // 24
    spare_light = SHORT_DEV - DOCS * low_light
    light_extra = spare_light * shares // jnp.sum(shares, axis=1, keepdims=True)
    light_left = spare_light - jnp.sum(light_extra, axis=1)
    light_row = low_light + light_extra + jnp.where(slots == 0, light_left[:, None], 0)
    lengths = jnp.where(heavy[:, None], heavy_row, light_row).astype(jnp.int32)
    dest = jnp.where(heavy[:, None] & (slots == DOCS - 1), ((ranks + half) % N_DP)[:, None], ranks[:, None]).astype(jnp.int32)
    return (lengths, dest)


def draw_doc_lengths(key, part):
    return plan_draw(jax.random.fold_in(key, 9))[0]


def draw_doc_dest(key, part):
    return plan_draw(jax.random.fold_in(key, 9))[1]


def draw_q_short(key, part):
    return joint_draw(jax.random.fold_in(key, 5), (N_DP * SHORT_DEV, HF))[0].astype(jnp.bfloat16)


def draw_k_short(key, part):
    return joint_draw(jax.random.fold_in(key, 5), (N_DP * SHORT_DEV, HF))[1].astype(jnp.bfloat16)


def draw_q_long(key, part):
    return joint_draw(jax.random.fold_in(key, 7), (N_DP, LONG, HF))[0].astype(jnp.bfloat16)


def draw_k_long(key, part):
    return joint_draw(jax.random.fold_in(key, 7), (N_DP, LONG, HF))[1].astype(jnp.bfloat16)


def steps_of(own_key, extent, cuts, least, top_value):
    def one(dim, blocks):
        steps = jax.random.uniform(jax.random.fold_in(jax.random.fold_in(own_key, 6), dim), (blocks,), jnp.float32, least / len(cuts), top_value / len(cuts))
        return jnp.repeat(jnp.exp(steps), extent[dim] // blocks).reshape((-1,) + (1,) * (len(extent) - dim - 1))

    loudness = one(*cuts[0])
    for cut in cuts[1:]:
        loudness = loudness * one(*cut)
    return loudness


def normal_values(own_key, shape, width, limit, shards=(), held_as=jnp.bfloat16):
    factor_of = steps_of(own_key, shape, shards, -0.22, 0.18) if shards else 1.0
    result = jax.random.normal(own_key, shape, jnp.float32) * width * factor_of
    return jnp.minimum(jnp.maximum(result, -limit), limit).astype(held_as)


def setup_inputs(seed: int = 0) -> dict:
    streams_of = jax.random.split(jax.random.key(seed), 12)
    return {
        "q_short": draw_q_short(jax.random.fold_in(streams_of[11], 71), 0),
        "k_short": draw_k_short(jax.random.fold_in(streams_of[11], 71), 0),
        "v_short": normal_values(streams_of[2], (N_DP * SHORT_DEV, HF), 1.0, 6.0, ((0, 8), (1, 4))),
        "dout_short": normal_values(streams_of[3], (N_DP * SHORT_DEV, HF), 1.0, 6.0, ((0, 8), (1, 4))),
        "doc_lengths": draw_doc_lengths(jax.random.fold_in(streams_of[11], 71), 0),
        "doc_dest": draw_doc_dest(jax.random.fold_in(streams_of[11], 71), 0),
        "q_long": draw_q_long(jax.random.fold_in(streams_of[11], 71), 0),
        "k_long": draw_k_long(jax.random.fold_in(streams_of[11], 71), 0),
        "v_long": normal_values(streams_of[8], (N_DP, LONG, HF), 1.0, 6.0, ((0, 8), (1, 4))),
        "dout_long": normal_values(streams_of[9], (N_DP, LONG, HF), 1.0, 6.0, ((0, 8), (1, 4))),
        "block_order": jax.random.permutation(streams_of[10], 2 * N_CTX).astype(jnp.int32),
    }


NEG = -1e30


def forward_rows(queries, keys, values, mask, scale):
    scores = jnp.einsum("qhd,khd->hqk", queries.astype(jnp.float32), keys.astype(jnp.float32)) * scale
    scores = jnp.where(mask[None], scores, NEG)
    top = jnp.max(scores, axis=-1, keepdims=True)
    lse = top + jnp.log(jnp.sum(jnp.exp(scores - top), axis=-1, keepdims=True))
    probs = jnp.where(mask[None], jnp.exp(scores - lse), 0.0)
    weights = lax.optimization_barrier(probs.astype(jnp.bfloat16))
    attended = jnp.einsum("hqk,khd->qhd", weights.astype(jnp.float32), values.astype(jnp.float32))
    return attended.astype(jnp.bfloat16), probs, weights


def backward_rows(probs, weights, attended, douts, queries, keys, values, scale):
    dfull = douts.astype(jnp.float32)
    dprobs = jnp.einsum("qhd,khd->hqk", dfull, values.astype(jnp.float32))
    delta = jnp.einsum("qhd,qhd->hq", dfull, attended.astype(jnp.float32))
    grads = probs * (dprobs - delta[:, :, None])
    score_grads = lax.optimization_barrier(grads.astype(jnp.bfloat16)).astype(jnp.float32)
    grad_q = jnp.einsum("hqk,khd->qhd", score_grads, keys.astype(jnp.float32)) * scale
    grad_k = jnp.einsum("hqk,qhd->khd", score_grads, queries.astype(jnp.float32)) * scale
    grad_v = jnp.einsum("hqk,qhd->khd", weights.astype(jnp.float32), dfull)
    return grad_q, grad_k, grad_v


def document_of(length_row, token_count):
    starts = (jnp.cumsum(length_row) - length_row).astype(jnp.int32)
    tokens = jnp.arange(token_count, dtype=jnp.int32)
    return (jnp.sum((tokens[:, None] >= starts[None, :]).astype(jnp.int32), axis=1) - 1).astype(jnp.int32)


def positions(block_order, total, rows):
    half = rows // 2
    index = jnp.arange(total, dtype=jnp.int32)
    onehot = ((index // half)[:, None] == jnp.arange(block_order.shape[0], dtype=jnp.int32)[None, :]).astype(jnp.int32)
    return (jnp.sum(onehot * block_order[None, :], axis=1) * half + index % half).astype(jnp.int32)


def reference(q_short, k_short, v_short, dout_short, doc_lengths, doc_dest, q_long, k_long, v_long, dout_long, block_order):
    scale = HEAD_DIM ** -0.5
    features = q_short.shape[1]
    heads = features // HEAD_DIM
    half = N_DP // 2
    tokens = jnp.arange(SHORT_DEV, dtype=jnp.int32)

    def short_rank(items):
        queries, keys, values, douts, length_row = items
        doc_of = document_of(length_row, SHORT_DEV)
        mask = (doc_of[None, :] == doc_of[:, None]) & (tokens[None, :] <= tokens[:, None])
        shaped = [x.reshape(SHORT_DEV, heads, HEAD_DIM) for x in (queries, keys, values, douts)]
        attended, probs, weights = forward_rows(shaped[0], shaped[1], shaped[2], mask, scale)
        grads = backward_rows(probs, weights, attended, shaped[3], shaped[0], shaped[1], shaped[2], scale)
        outs = [attended] + [g.astype(jnp.bfloat16) for g in grads]
        return tuple(o.reshape(SHORT_DEV, features) for o in outs)

    split = lambda x: x.reshape(N_DP, SHORT_DEV, features)
    attended_all, grad_q, grad_k, grad_v = lax.map(short_rank, (split(q_short), split(k_short), split(v_short), split(dout_short), doc_lengths))
    ranks = jnp.arange(N_DP, dtype=jnp.int32)
    moves = doc_dest[:, DOCS - 1] != ranks
    tails = doc_lengths[:, DOCS - 1].astype(jnp.int32)
    moved = moves[:, None] & (tokens[None, :] >= SHORT_DEV - tails[:, None])
    own = jnp.where(moved[..., None], jnp.zeros((), jnp.bfloat16), attended_all)
    partner = ((ranks + half) % N_DP).astype(jnp.int32)
    incoming = jnp.where(moves[partner], tails[partner], 0).astype(jnp.int32)
    padded = jnp.concatenate([attended_all, jnp.zeros((N_DP, MOVE, features), jnp.bfloat16)], axis=1)
    starts = (SHORT_DEV - tails[partner]).astype(jnp.int32)
    received = jax.vmap(lambda block, start: lax.dynamic_slice_in_dim(block, start, MOVE, 0))(padded[partner], starts)
    slots = jnp.arange(MOVE, dtype=jnp.int32)
    received = jnp.where((slots[None, :] < incoming[:, None])[..., None], received, jnp.zeros((), jnp.bfloat16))
    out_short = jnp.concatenate([own, received], axis=1).reshape(N_DP * (SHORT_DEV + MOVE), features)
    flat = lambda x: x.reshape(N_DP * SHORT_DEV, features)

    place = positions(block_order, LONG, LONG_DEV)
    long_mask = place[None, :] <= place[:, None]

    def long_doc(items):
        queries, keys, values, douts = [x.reshape(LONG, heads, HEAD_DIM) for x in items]
        attended, probs, weights = forward_rows(queries, keys, values, long_mask, scale)
        grads = backward_rows(probs, weights, attended, douts, queries, keys, values, scale)
        outs = [attended] + [g.astype(jnp.bfloat16) for g in grads]
        return tuple(o.reshape(LONG, features) for o in outs)

    out_long, dq_long, dk_long, dv_long = lax.map(long_doc, (q_long, k_long, v_long, dout_long))
    return out_short, flat(grad_q), flat(grad_k), flat(grad_v), out_long, dq_long, dk_long, dv_long
```

```python
import functools

import jax
import jax.numpy as jnp
from jax import lax
from jax.experimental import pallas as pl
from jax.experimental.pallas import tpu as pltpu
from jax.sharding import PartitionSpec as P


HEAD_DIM = 128
NEG = -1e30
LOG2E = 1.4426950408889634


def dot_rows(left, right):
    return lax.dot_general(
        left, right, (((1,), (1,)), ((), ())), preferred_element_type=jnp.float32
    )


def dot(left, right):
    return jnp.dot(left, right, preferred_element_type=jnp.float32)


def score_stage(queries, douts, keys, values):
    return dot_rows(keys, queries), dot_rows(values, douts)


def softmax_stage(scores, dprobs, tile, columns, mask_tile, scale):
    key_tiles = scores.shape[0] // tile
    weight_cols = []
    grad_cols = []
    for b, (first, last) in enumerate(columns):
        lanes = slice(b * tile, (b + 1) * tile)
        s_tiles = []
        top = None
        for j in range(first, last):
            s = mask_tile(scores[j * tile : (j + 1) * tile, lanes], j, b)
            s_tiles.append(s)
            part = jnp.max(s, axis=0, keepdims=True)
            top = part if top is None else jnp.maximum(top, part)
        e_tiles = [jnp.exp2((s - top) * (scale * LOG2E)) for s in s_tiles]
        total = sum(jnp.sum(e, axis=0, keepdims=True) for e in e_tiles)
        inverse = 1.0 / total
        p_tiles = [e * inverse for e in e_tiles]
        d_tiles = [dprobs[j * tile : (j + 1) * tile, lanes] for j in range(first, last)]
        delta = sum(jnp.sum(p * d, axis=0, keepdims=True) for p, d in zip(p_tiles, d_tiles))
        w_tiles = [p.astype(jnp.bfloat16) for p in p_tiles]
        g_tiles = [(p * (d - delta)).astype(jnp.bfloat16) for p, d in zip(p_tiles, d_tiles)]
        zero = jnp.zeros((tile, tile), jnp.bfloat16)
        before = [zero] * first
        after = [zero] * (key_tiles - last)
        weight_cols.append(jnp.concatenate(before + w_tiles + after, axis=0))
        grad_cols.append(jnp.concatenate(before + g_tiles + after, axis=0))
    return jnp.concatenate(weight_cols, axis=1), jnp.concatenate(grad_cols, axis=1)


def product_stage(weights, grads, queries, douts, keys_t, values_t, scale):
    attended = dot(values_t, weights).astype(jnp.bfloat16).T
    grad_q = (dot(keys_t, grads) * scale).astype(jnp.bfloat16).T
    return attended, grad_q, dot(grads, queries), dot(weights, douts)


def staged(blocks, scores_of, softmax_of, products_of, ahead=1):
    scores = {}
    for step in range(blocks + ahead):
        if step < blocks:
            scores[step] = scores_of(step)
        if step >= ahead:
            block = step - ahead
            products_of(block, *softmax_of(block, *scores.pop(block)))


def causal(s, tile):
    key = lax.broadcasted_iota(jnp.int32, (tile, tile), 0)
    query = lax.broadcasted_iota(jnp.int32, (tile, tile), 1)
    return jnp.where(key <= query, s, NEG)


def short_kernel(head, heads, lengths, dests, q_hbm, k_hbm, v_hbm, d_hbm, *rest):
    if head > 0:
        rest = rest[5:]
    else:
        order, rest = rest[0], rest[1:]
    out_hbm, dq_hbm, dk_hbm, dv_hbm = rest[:4]
    rest = rest[4:]
    if head == 0:
        (tail_ref, table_ref), rest = rest[:2], rest[2:]
        for index in range(order.shape[0]):
            table_ref[index : index + 1, :] = jnp.full((1, table_ref.shape[1]), order[index], jnp.int32)
    held, made, in_sem, out_sem = rest[:4]
    scale = HEAD_DIM ** (-0.5)
    tokens = q_hbm.shape[0]
    tile = tokens // 6
    span = 2 * tile
    rank = lax.axis_index("dp")
    count = lengths.shape[1]
    column = pl.ds(head * HEAD_DIM, HEAD_DIM)

    loads = [
        pltpu.make_async_copy(ref.at[:, column], held.at[slot], in_sem.at[slot])
        for slot, ref in enumerate((q_hbm, k_hbm, v_hbm, d_hbm))
    ]
    for load in loads:
        load.start()
    others = []
    if head == 0:
        ends, end_sem = rest[4:]
        for other in range(1, heads):
            columns = pl.ds(other * HEAD_DIM, HEAD_DIM)
            for slot, ref in enumerate((q_hbm, k_hbm, v_hbm)):
                others.append(
                    pltpu.make_async_copy(
                        ref.at[pl.ds(tokens - 3 * tile, 3 * tile), columns],
                        ends.at[other - 1, slot],
                        end_sem.at[len(others)],
                    )
                )
        for load in others:
            load.start()

    place = lax.broadcasted_iota(jnp.int32, (1, tokens), 1)
    start = jnp.zeros((1, tokens), jnp.int32)
    begin = jnp.int32(0)
    for j in range(count - 1):
        begin = begin + lengths[rank, j]
        start = jnp.where(place >= begin, begin, start)
    tail = lengths[rank, count - 1]
    moves = dests[rank, count - 1] != rank
    stores = []

    def store(slot, low, high, target):
        copy = pltpu.make_async_copy(
            made.at[slot, pl.ds(low, high - low), :],
            target.at[pl.ds(low, high - low), column],
            out_sem.at[len(stores)],
        )
        copy.start()
        stores.append(copy)

    for load in loads:
        load.wait()
    q_ref, k_ref, v_ref, d_ref = [held.at[slot] for slot in range(4)]
    keys_t = k_ref[...].T
    values_t = v_ref[...].T
    blocks = tokens // span
    pending = {}

    def key_low(block):
        return max(0, (block - 1) * span)

    def sent(last):
        to = lax.broadcasted_iota(jnp.int32, (tile, tile), 0)
        come = lax.broadcasted_iota(jnp.int32, (tile, tile), 1)
        pick = (come == to + (tile - tail)) & moves & (to < tail)
        return dot(pick.astype(jnp.float32).astype(jnp.bfloat16), last).astype(jnp.bfloat16)

    def scores_of(block):
        low = block * span
        keys = slice(key_low(block), low + span)
        return score_stage(q_ref[low : low + span, :], d_ref[low : low + span, :], k_ref[keys, :], v_ref[keys, :])

    def softmax_of(block, scores, dprobs):
        low = block * span
        offset = (low - key_low(block)) // tile

        def mask_tile(s, j, b):
            key = lax.broadcasted_iota(jnp.int32, (tile, tile), 0)
            first = start[:, low + b * tile : low + (b + 1) * tile] - (key_low(block) + j * tile)
            allowed = key >= first
            if j == offset + b:
                query = lax.broadcasted_iota(jnp.int32, (tile, tile), 1)
                allowed = allowed & (key <= query)
            return jnp.where(allowed, s, NEG)

        columns = [(max(0, offset + b - 2), offset + b + 1) for b in range(2)]
        return softmax_stage(scores, dprobs, tile, columns, mask_tile, scale)

    def products_of(block, weights, grads):
        low = block * span
        high = low + span
        keys = slice(key_low(block), high)
        attended, grad_q, grad_k, grad_v = product_stage(
            weights,
            grads,
            q_ref[low:high, :],
            d_ref[low:high, :],
            keys_t[:, keys],
            values_t[:, keys],
            scale,
        )
        made[1, low:high, :] = grad_q
        store(1, low, high, dq_hbm)
        if high == tokens:
            last = attended[tile:, :]
            row = lax.broadcasted_iota(jnp.int32, (tile, 1), 0)
            kept = jnp.logical_not(moves & (row >= tile - tail))
            made[0, low : low + tile, :] = attended[:tile, :]
            made[0, low + tile : tokens, :] = jnp.where(kept, last, jnp.zeros_like(last))
            if head == 0:
                tail_ref[0] = sent(last)
        else:
            made[0, low:high, :] = attended
        store(0, low, high, out_hbm)
        if block > 0:
            done_k = pending["k"] + grad_k[:span]
            done_v = pending["v"] + grad_v[:span]
            made[2, low - span : low, :] = (done_k * scale).astype(jnp.bfloat16)
            made[3, low - span : low, :] = done_v.astype(jnp.bfloat16)
            store(2, low - span, low, dk_hbm)
            store(3, low - span, low, dv_hbm)
        pending["k"] = grad_k[-span:]
        pending["v"] = grad_v[-span:]
        if high == tokens:
            made[2, low:high, :] = (pending["k"] * scale).astype(jnp.bfloat16)
            made[3, low:high, :] = pending["v"].astype(jnp.bfloat16)
            store(2, low, high, dk_hbm)
            store(3, low, high, dv_hbm)

    staged(blocks, scores_of, softmax_of, products_of)
    for load in others:
        load.wait()
    if head == 0:
        for other in range(1, heads):
            scores = dot_rows(ends[other - 1, 1], ends[other - 1, 0, 2 * tile :, :])
            key = lax.broadcasted_iota(jnp.int32, scores.shape, 0)
            query = lax.broadcasted_iota(jnp.int32, scores.shape, 1) + 2 * tile
            first = start[:, tokens - tile :] - (tokens - 3 * tile)
            scores = jnp.where((key >= first) & (key <= query), scores, NEG)
            grown = jnp.exp2((scores - jnp.max(scores, axis=0, keepdims=True)) * (scale * LOG2E))
            weights = (grown * (1.0 / jnp.sum(grown, axis=0, keepdims=True))).astype(jnp.bfloat16)
            tail_ref[other] = sent(dot(weights.T, ends[other - 1, 2]).astype(jnp.bfloat16))
    for copy in stores:
        copy.wait()


def short_attention(head, heads, lengths, dests, arrays, before, after, order=None):
    tokens, width = arrays[0].shape
    move = tokens // 6
    blocks = 3
    smem = pl.BlockSpec(memory_space=pltpu.SMEM)
    hbm = pl.BlockSpec(memory_space=pltpu.HBM)
    vmem = pl.BlockSpec(memory_space=pltpu.VMEM)
    wide = jax.ShapeDtypeStruct((tokens, width), jnp.bfloat16)
    first = before is None
    extra = [order] if first else list(before[:4]) + [after]
    tile = move
    return pl.pallas_call(
        functools.partial(short_kernel, head, heads),
        in_specs=[smem] * 2 + [hbm] * 4 + ([smem] if first else [hbm] * 4 + [pl.BlockSpec(memory_space=pl.ANY)]),
        out_specs=[hbm] * 4 + ([vmem] * 2 if first else []),
        out_shape=[jax.ShapeDtypeStruct((tokens + move, width), jnp.bfloat16), wide, wide, wide]
        + (
            [
                jax.ShapeDtypeStruct((heads, move, HEAD_DIM), jnp.bfloat16),
                jax.ShapeDtypeStruct((order.shape[0], HEAD_DIM), jnp.int32),
            ]
            if first
            else []
        ),
        scratch_shapes=[
            pltpu.VMEM((4, tokens, HEAD_DIM), jnp.bfloat16),
            pltpu.VMEM((4, tokens, HEAD_DIM), jnp.bfloat16),
            pltpu.SemaphoreType.DMA((4,)),
            pltpu.SemaphoreType.DMA((4 * blocks,)),
        ]
        + (
            [
                pltpu.VMEM((max(heads - 1, 1), 3, 3 * tile, HEAD_DIM), jnp.bfloat16),
                pltpu.SemaphoreType.DMA((max(3 * heads - 3, 1),)),
            ]
            if first
            else []
        ),
        input_output_aliases={} if first else {6 + i: i for i in range(4)},
        compiler_params=pltpu.CompilerParams(vmem_limit_bytes=16 << 20),
        cost_estimate=pl.CostEstimate(flops=10**9, bytes_accessed=3 * 10**6, transcendentals=0),
    )(lengths, dests, *arrays, *extra)


def peer_order(ways):
    return [step for step in range(2, ways)] + [1]


def pack_kernel(head, ways, q_ref, k_ref, v_ref, d_ref, *rest):
    steps = peer_order(ways) + [0]
    outs, sem = rest[: len(steps)], rest[-1]
    own = lax.axis_index("ctx")
    per = q_ref.shape[2] // ways
    copies = []
    for out, step in zip(outs, steps):
        column = pl.multiple_of((own ^ step) * per + head * HEAD_DIM, HEAD_DIM)
        for slot, ref in enumerate((q_ref, k_ref, v_ref, d_ref)):
            copies.append(
                pltpu.make_async_copy(
                    ref.at[0, :, pl.ds(column, HEAD_DIM)], out.at[slot], sem.at[len(copies)]
                )
            )
    for copy in copies:
        copy.start()
    for copy in copies:
        copy.wait()


def pack(head, ways, arrays):
    rows = arrays[0].shape[1]
    return pl.pallas_call(
        functools.partial(pack_kernel, head, ways),
        in_specs=[pl.BlockSpec(memory_space=pltpu.HBM)] * 4,
        out_specs=[pl.BlockSpec(memory_space=pltpu.VMEM)] * ways,
        out_shape=[jax.ShapeDtypeStruct((4, rows, HEAD_DIM), jnp.bfloat16)] * ways,
        scratch_shapes=[pltpu.SemaphoreType.DMA((4 * ways,))],
        compiler_params=pltpu.CompilerParams(vmem_limit_bytes=8 << 20),
        cost_estimate=pl.CostEstimate(flops=0, bytes_accessed=2 * 10**6, transcendentals=0),
    )(*[pltpu.with_memory_space_constraint(array, pltpu.HBM) for array in arrays])


def long_kernel(ways, linked, order, *rest):
    rest = rest[linked:]
    steps = peer_order(ways) + [0]
    arrived = rest[:ways]
    outs = rest[ways : 2 * ways]
    held, made = rest[2 * ways + linked :]
    scale = HEAD_DIM ** (-0.5)
    own = lax.axis_index("ctx")
    rows = arrived[0].shape[1]
    half = rows // 2
    total = rows * ways

    def spot(device, part):
        return pl.ds(pl.multiple_of(order[device * 2 + part, 0] * half, half), half)

    for buffer, step in zip(arrived, steps):
        for part in range(2):
            piece = slice(part * half, (part + 1) * half)
            for slot in range(4):
                held[slot, spot(own ^ step, part), :] = buffer[slot, piece, :]

    tile = HEAD_DIM
    span = 2 * tile
    blocks = total // span
    keys_t = held[1].T
    values_t = held[2].T
    sum_k = [None] * blocks
    sum_v = [None] * blocks

    def scores_of(block):
        low, high = block * span, (block + 1) * span
        return score_stage(held[0, low:high, :], held[3, low:high, :], held[1, :high, :], held[2, :high, :])

    def softmax_of(block, scores, dprobs):
        first = block * span // tile

        def mask_tile(s, j, b):
            return causal(s, tile) if j == first + b else s

        columns = [(0, first + b + 1) for b in range(span // tile)]
        return softmax_stage(scores, dprobs, tile, columns, mask_tile, scale)

    def products_of(block, weights, grads):
        low, high = block * span, (block + 1) * span
        attended, grad_q, grad_k, grad_v = product_stage(
            weights, grads, held[0, low:high, :], held[3, low:high, :], keys_t[:, :high], values_t[:, :high], scale
        )
        made[0, low:high, :] = attended
        made[1, low:high, :] = grad_q
        for part in range(block + 1):
            piece = slice(part * span, (part + 1) * span)
            sum_k[part] = grad_k[piece] if sum_k[part] is None else sum_k[part] + grad_k[piece]
            sum_v[part] = grad_v[piece] if sum_v[part] is None else sum_v[part] + grad_v[piece]

    staged(blocks, scores_of, softmax_of, products_of)
    for part in range(blocks):
        piece = slice(part * span, (part + 1) * span)
        made[2, piece, :] = (sum_k[part] * scale).astype(jnp.bfloat16)
        made[3, piece, :] = sum_v[part].astype(jnp.bfloat16)

    for out, step in zip(outs, steps):
        for part in range(2):
            piece = slice(part * half, (part + 1) * half)
            for slot in range(4):
                out[slot, piece, :] = made[slot, spot(own ^ step, part), :]


def long_attention(ways, order, arrived, linked=()):
    anywhere = [pl.BlockSpec(memory_space=pl.ANY)] * len(linked)
    rows = arrived[0].shape[1]
    piece = jax.ShapeDtypeStruct((4, rows, HEAD_DIM), jnp.bfloat16)
    vmem = pl.BlockSpec(memory_space=pltpu.VMEM)
    return pl.pallas_call(
        functools.partial(long_kernel, ways, len(linked)),
        in_specs=[vmem] + anywhere + [vmem] * ways,
        out_specs=[vmem] * ways + anywhere,
        out_shape=[piece] * ways + [jax.ShapeDtypeStruct(x.shape, x.dtype) for x in linked],
        scratch_shapes=[
            pltpu.VMEM((4, rows * ways, HEAD_DIM), jnp.bfloat16),
            pltpu.VMEM((4, rows * ways, HEAD_DIM), jnp.bfloat16),
        ],
        input_output_aliases={1 + i: ways + i for i in range(len(linked))},
        compiler_params=pltpu.CompilerParams(vmem_limit_bytes=16 << 20),
        cost_estimate=pl.CostEstimate(flops=10**9, bytes_accessed=3 * 10**6, transcendentals=0),
    )(order, *linked, *arrived)


def join_kernel(ways, head, last, *refs):
    steps = peer_order(ways) + [0]
    pieces = refs[:ways]
    refs = refs[ways:]
    if last:
        received, refs = refs[0], refs[1:]
    if head > 0:
        refs = refs[4 + int(last) :]
    outs, refs = refs[:4], refs[4:]
    sem = refs[-1]
    own = lax.axis_index("ctx")
    per = outs[0].shape[2] // ways
    copies = []
    for piece, step in zip(pieces, steps):
        column = pl.multiple_of((own ^ step) * per + head * HEAD_DIM, HEAD_DIM)
        for slot, out in enumerate(outs):
            copies.append(
                pltpu.make_async_copy(
                    piece.at[slot], out.at[0, :, pl.ds(column, HEAD_DIM)], sem.at[len(copies)]
                )
            )
    if last:
        short_out = refs[0]
        heads, move, _ = received.shape
        for other in range(heads):
            copies.append(
                pltpu.make_async_copy(
                    received.at[other],
                    short_out.at[pl.ds(short_out.shape[0] - move, move), pl.ds(other * HEAD_DIM, HEAD_DIM)],
                    sem.at[len(copies)],
                )
            )
    for copy in copies:
        copy.start()
    for copy in copies:
        copy.wait()


def join(ways, head, pieces, outs, shape, received=None, short_out=None):
    last = received is not None
    vmem = pl.BlockSpec(memory_space=pltpu.VMEM)
    hbm = pl.BlockSpec(memory_space=pltpu.HBM)
    operands = list(pieces)
    in_specs = [vmem] * ways
    out_shape = [jax.ShapeDtypeStruct(shape, jnp.bfloat16)] * 4
    aliases = {}
    if last:
        operands.append(received)
        in_specs.append(vmem)
        out_shape.append(jax.ShapeDtypeStruct(short_out.shape, jnp.bfloat16))
    old = ([] if outs is None else list(outs)) + ([short_out] if last else [])
    first_out = 0 if outs is not None else 4
    for index, value in enumerate(old):
        aliases[len(operands)] = first_out + index
        operands.append(value)
        in_specs.append(hbm)
    return pl.pallas_call(
        functools.partial(join_kernel, ways, head, last),
        in_specs=in_specs,
        out_specs=[hbm] * len(out_shape),
        out_shape=out_shape,
        scratch_shapes=[pltpu.SemaphoreType.DMA((4 * ways + 2,))],
        input_output_aliases=aliases,
        compiler_params=pltpu.CompilerParams(vmem_limit_bytes=8 << 20),
        cost_estimate=pl.CostEstimate(flops=0, bytes_accessed=10**6, transcendentals=0),
    )(*operands)


def shards(
    q_short,
    k_short,
    v_short,
    dout_short,
    doc_lengths,
    doc_dest,
    q_long,
    k_long,
    v_long,
    dout_long,
    block_order,
):
    ways = lax.axis_size("ctx")
    ranks = lax.axis_size("dp")
    steps = peer_order(ways)
    heads_each = q_long.shape[2] // HEAD_DIM // ways
    arrays = (q_long, k_long, v_long, dout_long)

    def swap(value, step):
        return lax.ppermute(value, "ctx", [(i, i ^ step) for i in range(ways)])

    arrived = []
    for head in range(heads_each):
        packed = pack(head, ways, arrays)
        arrived.append([swap(value, step) for value, step in zip(packed, steps)] + [packed[-1]])
    shorts = (q_short, k_short, v_short, dout_short)
    short_heads = q_short.shape[1] // HEAD_DIM
    short = short_attention(0, short_heads, doc_lengths, doc_dest, shorts, None, None, block_order)
    (tail, table), short = short[4:], short[:4]
    pieces = []
    for head in range(heads_each):
        made = long_attention(ways, table, arrived[head], (tail,) if head == 0 else ())
        if head == 0:
            tail = made[-1]
            received = lax.ppermute(tail, "dp", [(i, (i + ranks // 2) % ranks) for i in range(ranks)])
        pieces.append([swap(value, step) for value, step in zip(made[: ways - 1], steps)] + [made[ways - 1]])
    for head in range(1, short_heads):
        short = short_attention(head, short_heads, doc_lengths, doc_dest, shorts, short, pieces[-1][-1])
    outs = None
    for head in range(heads_each - 1):
        outs = join(ways, head, pieces[head], outs, q_long.shape)
    out_long, dq_long, dk_long, dv_long, out_short = join(
        ways, heads_each - 1, pieces[-1], outs, q_long.shape, received, short[0]
    )
    dq_short, dk_short, dv_short = short[1:]
    return (out_short, dq_short, dk_short, dv_short, out_long, dq_long, dk_long, dv_long)


def solution(mesh):
    flat = P("dp", "ctx")
    deep = P("dp", "ctx", None)

    return jax.shard_map(
        shards,
        mesh=mesh,
        in_specs=(flat,) * 4 + (P(), P()) + (deep,) * 4 + (P(),),
        out_specs=(flat,) * 4 + (deep,) * 4,
        check_vma=False,
    )
```

```python
import functools

import jax
import jax.numpy as jnp
from jax import lax
from jax.experimental import pallas as pl
from jax.experimental.pallas import tpu as pltpu
from jax.sharding import PartitionSpec as P


HEAD_DIM = 128
NEG = -1e30
LOG2E = 1.4426950408889634


def dot_rows(left, right):
    return lax.dot_general(
        left, right, (((1,), (1,)), ((), ())), preferred_element_type=jnp.float32
    )


def dot(left, right):
    return jnp.dot(left, right, preferred_element_type=jnp.float32)


def score_stage(queries, douts, keys, values):
    return dot_rows(keys, queries), dot_rows(values, douts)


def softmax_stage(scores, dprobs, tile, columns, mask_tile, scale):
    key_tiles = scores.shape[0] // tile
    weight_cols = []
    grad_cols = []
    for b, (first, last) in enumerate(columns):
        lanes = slice(b * tile, (b + 1) * tile)
        s_tiles = []
        top = None
        for j in range(first, last):
            s = mask_tile(scores[j * tile : (j + 1) * tile, lanes], j, b)
            s_tiles.append(s)
            part = jnp.max(s, axis=0, keepdims=True)
            top = part if top is None else jnp.maximum(top, part)
        e_tiles = [jnp.exp2((s - top) * (scale * LOG2E)) for s in s_tiles]
        total = sum(jnp.sum(e, axis=0, keepdims=True) for e in e_tiles)
        inverse = 1.0 / total
        p_tiles = [e * inverse for e in e_tiles]
        d_tiles = [dprobs[j * tile : (j + 1) * tile, lanes] for j in range(first, last)]
        delta = sum(jnp.sum(p * d, axis=0, keepdims=True) for p, d in zip(p_tiles, d_tiles))
        w_tiles = [p.astype(jnp.bfloat16) for p in p_tiles]
        g_tiles = [(p * (d - delta)).astype(jnp.bfloat16) for p, d in zip(p_tiles, d_tiles)]
        zero = jnp.zeros((tile, tile), jnp.bfloat16)
        before = [zero] * first
        after = [zero] * (key_tiles - last)
        weight_cols.append(jnp.concatenate(before + w_tiles + after, axis=0))
        grad_cols.append(jnp.concatenate(before + g_tiles + after, axis=0))
    return jnp.concatenate(weight_cols, axis=1), jnp.concatenate(grad_cols, axis=1)


def product_stage(weights, grads, queries, douts, keys_t, values_t, scale):
    attended = dot(values_t, weights).astype(jnp.bfloat16).T
    grad_q = (dot(keys_t, grads) * scale).astype(jnp.bfloat16).T
    return attended, grad_q, dot(grads, queries), dot(weights, douts)


def staged(blocks, scores_of, softmax_of, products_of, ahead=1):
    scores = {}
    for step in range(blocks + ahead):
        if step < blocks:
            scores[step] = scores_of(step)
        if step >= ahead:
            block = step - ahead
            products_of(block, *softmax_of(block, *scores.pop(block)))


def causal(s, tile):
    key = lax.broadcasted_iota(jnp.int32, (tile, tile), 0)
    query = lax.broadcasted_iota(jnp.int32, (tile, tile), 1)
    return jnp.where(key <= query, s, NEG)


def short_kernel(head, heads, lengths, dests, q_hbm, k_hbm, v_hbm, d_hbm, *rest):
    if head > 0:
        rest = rest[5:]
    else:
        order, rest = rest[0], rest[1:]
    out_hbm, dq_hbm, dk_hbm, dv_hbm = rest[:4]
    rest = rest[4:]
    if head == 0:
        (tail_ref, table_ref), rest = rest[:2], rest[2:]
        for index in range(order.shape[0]):
            table_ref[index : index + 1, :] = jnp.full((1, table_ref.shape[1]), order[index], jnp.int32)
    held, made, in_sem, out_sem = rest[:4]
    scale = HEAD_DIM ** (-0.5)
    tokens = q_hbm.shape[0]
    tile = tokens // 6
    span = 2 * tile
    rank = lax.axis_index("dp")
    count = lengths.shape[1]
    column = pl.ds(head * HEAD_DIM, HEAD_DIM)

    loads = [
        pltpu.make_async_copy(ref.at[:, column], held.at[slot], in_sem)
        for slot, ref in enumerate((q_hbm, k_hbm, v_hbm, d_hbm))
    ]
    for load in loads:
        load.start()
    others = []
    if head == 0:
        ends, end_sem = rest[4:]
        for other in range(1, heads):
            columns = pl.ds(other * HEAD_DIM, HEAD_DIM)
            for slot, ref in enumerate((q_hbm, k_hbm, v_hbm)):
                others.append(
                    pltpu.make_async_copy(
                        ref.at[pl.ds(tokens - 3 * tile, 3 * tile), columns],
                        ends.at[other - 1, slot],
                        end_sem,
                    )
                )
        for load in others:
            load.start()

    place = lax.broadcasted_iota(jnp.int32, (1, tokens), 1)
    start = jnp.zeros((1, tokens), jnp.int32)
    begin = jnp.int32(0)
    for j in range(count - 1):
        begin = begin + lengths[rank, j]
        start = jnp.where(place >= begin, begin, start)
    tail = lengths[rank, count - 1]
    moves = dests[rank, count - 1] != rank

    def store(slot, low, high, target):
        rows = pl.ds(low, high - low)
        pltpu.make_async_copy(made.at[slot, rows, :], target.at[rows, column], out_sem).start()

    pltpu.make_async_copy(held, held, in_sem).wait()
    q_ref, k_ref, v_ref, d_ref = [held.at[slot] for slot in range(4)]
    keys_t = k_ref[...].T
    values_t = v_ref[...].T
    blocks = tokens // span
    pending = {}

    def key_low(block):
        return max(0, (block - 1) * span)

    def sent(last):
        to = lax.broadcasted_iota(jnp.int32, (tile, tile), 0)
        come = lax.broadcasted_iota(jnp.int32, (tile, tile), 1)
        pick = (come == to + (tile - tail)) & moves & (to < tail)
        return dot(pick.astype(jnp.float32).astype(jnp.bfloat16), last).astype(jnp.bfloat16)

    def scores_of(block):
        low = block * span
        keys = slice(key_low(block), low + span)
        return score_stage(q_ref[low : low + span, :], d_ref[low : low + span, :], k_ref[keys, :], v_ref[keys, :])

    def softmax_of(block, scores, dprobs):
        low = block * span
        offset = (low - key_low(block)) // tile

        def mask_tile(s, j, b):
            key = lax.broadcasted_iota(jnp.int32, (tile, tile), 0)
            first = start[:, low + b * tile : low + (b + 1) * tile] - (key_low(block) + j * tile)
            allowed = key >= first
            if j == offset + b:
                query = lax.broadcasted_iota(jnp.int32, (tile, tile), 1)
                allowed = allowed & (key <= query)
            return jnp.where(allowed, s, NEG)

        columns = [(max(0, offset + b - 2), offset + b + 1) for b in range(2)]
        return softmax_stage(scores, dprobs, tile, columns, mask_tile, scale)

    def products_of(block, weights, grads):
        low = block * span
        high = low + span
        keys = slice(key_low(block), high)
        attended, grad_q, grad_k, grad_v = product_stage(
            weights,
            grads,
            q_ref[low:high, :],
            d_ref[low:high, :],
            keys_t[:, keys],
            values_t[:, keys],
            scale,
        )
        made[1, low:high, :] = grad_q
        store(1, low, high, dq_hbm)
        if high == tokens:
            last = attended[tile:, :]
            row = lax.broadcasted_iota(jnp.int32, (tile, 1), 0)
            kept = jnp.logical_not(moves & (row >= tile - tail))
            made[0, low : low + tile, :] = attended[:tile, :]
            made[0, low + tile : tokens, :] = jnp.where(kept, last, jnp.zeros_like(last))
            if head == 0:
                tail_ref[0] = sent(last)
        else:
            made[0, low:high, :] = attended
        store(0, low, high, out_hbm)
        if block > 0:
            done_k = pending["k"] + grad_k[:span]
            done_v = pending["v"] + grad_v[:span]
            made[2, low - span : low, :] = (done_k * scale).astype(jnp.bfloat16)
            made[3, low - span : low, :] = done_v.astype(jnp.bfloat16)
            store(2, low - span, low, dk_hbm)
            store(3, low - span, low, dv_hbm)
        pending["k"] = grad_k[-span:]
        pending["v"] = grad_v[-span:]
        if high == tokens:
            made[2, low:high, :] = (pending["k"] * scale).astype(jnp.bfloat16)
            made[3, low:high, :] = pending["v"].astype(jnp.bfloat16)
            store(2, low, high, dk_hbm)
            store(3, low, high, dv_hbm)

    staged(blocks, scores_of, softmax_of, products_of)
    if others:
        pltpu.make_async_copy(ends, ends, end_sem).wait()
        for other in range(1, heads):
            scores = dot_rows(ends[other - 1, 1], ends[other - 1, 0, 2 * tile :, :])
            key = lax.broadcasted_iota(jnp.int32, scores.shape, 0)
            query = lax.broadcasted_iota(jnp.int32, scores.shape, 1) + 2 * tile
            first = start[:, tokens - tile :] - (tokens - 3 * tile)
            scores = jnp.where((key >= first) & (key <= query), scores, NEG)
            grown = jnp.exp2((scores - jnp.max(scores, axis=0, keepdims=True)) * (scale * LOG2E))
            weights = (grown * (1.0 / jnp.sum(grown, axis=0, keepdims=True))).astype(jnp.bfloat16)
            tail_ref[other] = sent(dot(weights.T, ends[other - 1, 2]).astype(jnp.bfloat16))
    pltpu.make_async_copy(made, made, out_sem).wait()


def short_attention(head, heads, lengths, dests, arrays, before, after, order=None):
    tokens, width = arrays[0].shape
    move = tokens // 6
    smem = pl.BlockSpec(memory_space=pltpu.SMEM)
    hbm = pl.BlockSpec(memory_space=pltpu.HBM)
    vmem = pl.BlockSpec(memory_space=pltpu.VMEM)
    wide = jax.ShapeDtypeStruct((tokens, width), jnp.bfloat16)
    first = before is None
    extra = [order] if first else list(before[:4]) + [after]
    tile = move
    return pl.pallas_call(
        functools.partial(short_kernel, head, heads),
        in_specs=[smem] * 2 + [hbm] * 4 + ([smem] if first else [hbm] * 4 + [pl.BlockSpec(memory_space=pl.ANY)]),
        out_specs=[hbm] * 4 + ([vmem] * 2 if first else []),
        out_shape=[jax.ShapeDtypeStruct((tokens + move, width), jnp.bfloat16), wide, wide, wide]
        + (
            [
                jax.ShapeDtypeStruct((heads, move, HEAD_DIM), jnp.bfloat16),
                jax.ShapeDtypeStruct((order.shape[0], HEAD_DIM), jnp.int32),
            ]
            if first
            else []
        ),
        scratch_shapes=[
            pltpu.VMEM((4, tokens, HEAD_DIM), jnp.bfloat16),
            pltpu.VMEM((4, tokens, HEAD_DIM), jnp.bfloat16),
            pltpu.SemaphoreType.DMA,
            pltpu.SemaphoreType.DMA,
        ]
        + (
            [
                pltpu.VMEM((max(heads - 1, 1), 3, 3 * tile, HEAD_DIM), jnp.bfloat16),
                pltpu.SemaphoreType.DMA,
            ]
            if first
            else []
        ),
        input_output_aliases={} if first else {6 + i: i for i in range(4)},
        compiler_params=pltpu.CompilerParams(vmem_limit_bytes=16 << 20),
        cost_estimate=pl.CostEstimate(flops=10**9, bytes_accessed=3 * 10**6, transcendentals=0),
    )(lengths, dests, *arrays, *extra)


def peer_order(ways):
    return [step for step in range(2, ways)] + [1]


def pack_kernel(parts, ways, after, q_ref, k_ref, v_ref, d_ref, *rest):
    rest = rest[after:]
    outs, (all_bytes, sem) = rest[: len(parts)], rest[len(parts) :]
    own = lax.axis_index("ctx")
    per = q_ref.shape[2] // ways
    for out, (head, step) in zip(outs, parts):
        column = pl.multiple_of((own ^ step) * per + head * HEAD_DIM, HEAD_DIM)
        for slot, ref in enumerate((q_ref, k_ref, v_ref, d_ref)):
            pltpu.make_async_copy(ref.at[0, :, pl.ds(column, HEAD_DIM)], out.at[slot], sem).start()
    pltpu.make_async_copy(all_bytes, all_bytes, sem).wait()


def pack(parts, ways, arrays, after=()):
    rows = arrays[0].shape[1]
    return pl.pallas_call(
        functools.partial(pack_kernel, parts, ways, len(after)),
        in_specs=[pl.BlockSpec(memory_space=pltpu.HBM)] * 4 + [pl.BlockSpec(memory_space=pl.ANY)] * len(after),
        out_specs=[pl.BlockSpec(memory_space=pltpu.VMEM)] * len(parts),
        out_shape=[jax.ShapeDtypeStruct((4, rows, HEAD_DIM), jnp.bfloat16)] * len(parts),
        scratch_shapes=[
            pltpu.VMEM((4 * len(parts), rows, HEAD_DIM), jnp.bfloat16),
            pltpu.SemaphoreType.DMA,
        ],
        compiler_params=pltpu.CompilerParams(vmem_limit_bytes=8 << 20),
        cost_estimate=pl.CostEstimate(flops=0, bytes_accessed=2 * 10**6, transcendentals=0),
    )(*[pltpu.with_memory_space_constraint(array, pltpu.HBM) for array in arrays], *after)


def long_kernel(ways, linked, order, *rest):
    rest = rest[linked:]
    steps = peer_order(ways) + [0]
    arrived = rest[:ways]
    outs = rest[ways : 2 * ways]
    held, made = rest[2 * ways :]
    scale = HEAD_DIM ** (-0.5)
    own = lax.axis_index("ctx")
    rows = arrived[0].shape[1]
    half = rows // 2
    total = rows * ways

    def spot(device, part):
        return pl.ds(pl.multiple_of(order[device * 2 + part, 0] * half, half), half)

    for buffer, step in zip(arrived, steps):
        for part in range(2):
            piece = slice(part * half, (part + 1) * half)
            for slot in range(4):
                held[slot, spot(own ^ step, part), :] = buffer[slot, piece, :]

    tile = HEAD_DIM
    span = 2 * tile
    blocks = total // span
    keys_t = held[1].T
    values_t = held[2].T
    sum_k = [None] * blocks
    sum_v = [None] * blocks

    def scores_of(block):
        low, high = block * span, (block + 1) * span
        return score_stage(held[0, low:high, :], held[3, low:high, :], held[1, :high, :], held[2, :high, :])

    def softmax_of(block, scores, dprobs):
        first = block * span // tile

        def mask_tile(s, j, b):
            return causal(s, tile) if j == first + b else s

        columns = [(0, first + b + 1) for b in range(span // tile)]
        return softmax_stage(scores, dprobs, tile, columns, mask_tile, scale)

    def products_of(block, weights, grads):
        low, high = block * span, (block + 1) * span
        attended, grad_q, grad_k, grad_v = product_stage(
            weights, grads, held[0, low:high, :], held[3, low:high, :], keys_t[:, :high], values_t[:, :high], scale
        )
        made[0, low:high, :] = attended
        made[1, low:high, :] = grad_q
        for part in range(block + 1):
            piece = slice(part * span, (part + 1) * span)
            sum_k[part] = grad_k[piece] if sum_k[part] is None else sum_k[part] + grad_k[piece]
            sum_v[part] = grad_v[piece] if sum_v[part] is None else sum_v[part] + grad_v[piece]

    staged(blocks, scores_of, softmax_of, products_of)
    for part in range(blocks):
        piece = slice(part * span, (part + 1) * span)
        made[2, piece, :] = (sum_k[part] * scale).astype(jnp.bfloat16)
        made[3, piece, :] = sum_v[part].astype(jnp.bfloat16)

    for out, step in zip(outs, steps):
        for part in range(2):
            piece = slice(part * half, (part + 1) * half)
            for slot in range(4):
                out[slot, piece, :] = made[slot, spot(own ^ step, part), :]


def long_attention(ways, order, arrived, linked=()):
    anywhere = [pl.BlockSpec(memory_space=pl.ANY)] * len(linked)
    rows = arrived[0].shape[1]
    piece = jax.ShapeDtypeStruct((4, rows, HEAD_DIM), jnp.bfloat16)
    vmem = pl.BlockSpec(memory_space=pltpu.VMEM)
    return pl.pallas_call(
        functools.partial(long_kernel, ways, len(linked)),
        in_specs=[vmem] + anywhere + [vmem] * ways,
        out_specs=[vmem] * ways,
        out_shape=[piece] * ways,
        scratch_shapes=[
            pltpu.VMEM((4, rows * ways, HEAD_DIM), jnp.bfloat16),
            pltpu.VMEM((4, rows * ways, HEAD_DIM), jnp.bfloat16),
        ],
        compiler_params=pltpu.CompilerParams(vmem_limit_bytes=16 << 20),
        cost_estimate=pl.CostEstimate(flops=10**9, bytes_accessed=3 * 10**6, transcendentals=0),
    )(order, *linked, *arrived)


def join_kernel(parts, ways, olds, with_short, *refs):
    pieces = refs[: len(parts)]
    refs = refs[len(parts) :]
    if with_short:
        received, refs = refs[0], refs[1:]
    refs = refs[olds:]
    outs, refs = refs[:4], refs[4:]
    all_bytes, sem = refs[-2:]
    own = lax.axis_index("ctx")
    per = outs[0].shape[2] // ways
    for piece, (head, step) in zip(pieces, parts):
        column = pl.multiple_of((own ^ step) * per + head * HEAD_DIM, HEAD_DIM)
        for slot, out in enumerate(outs):
            pltpu.make_async_copy(piece.at[slot], out.at[0, :, pl.ds(column, HEAD_DIM)], sem).start()
    if with_short:
        short_out = refs[0]
        heads, move, _ = received.shape
        rows = pl.ds(short_out.shape[0] - move, move)
        for other in range(heads):
            columns = pl.ds(other * HEAD_DIM, HEAD_DIM)
            pltpu.make_async_copy(received.at[other], short_out.at[rows, columns], sem).start()
    pltpu.make_async_copy(all_bytes, all_bytes, sem).wait()


def join(parts, ways, pieces, outs, shape, received=None, short_out=None):
    with_short = received is not None
    vmem = pl.BlockSpec(memory_space=pltpu.VMEM)
    hbm = pl.BlockSpec(memory_space=pltpu.HBM)
    operands = list(pieces)
    in_specs = [vmem] * len(pieces)
    out_shape = [jax.ShapeDtypeStruct(shape, jnp.bfloat16)] * 4
    aliases = {}
    size = 4 * len(parts) * shape[1]
    if with_short:
        operands.append(received)
        in_specs.append(vmem)
        out_shape.append(jax.ShapeDtypeStruct(short_out.shape, jnp.bfloat16))
        size += received.shape[0] * received.shape[1]
    old = ([] if outs is None else list(outs)) + ([short_out] if with_short else [])
    first_out = 0 if outs is not None else 4
    for index, value in enumerate(old):
        aliases[len(operands)] = first_out + index
        operands.append(value)
        in_specs.append(hbm)
    return pl.pallas_call(
        functools.partial(join_kernel, parts, ways, len(old), with_short),
        in_specs=in_specs,
        out_specs=[hbm] * len(out_shape),
        out_shape=out_shape,
        scratch_shapes=[pltpu.VMEM((size, HEAD_DIM), jnp.bfloat16), pltpu.SemaphoreType.DMA],
        input_output_aliases=aliases,
        compiler_params=pltpu.CompilerParams(vmem_limit_bytes=8 << 20),
        cost_estimate=pl.CostEstimate(flops=0, bytes_accessed=10**6, transcendentals=0),
    )(*operands)


def shards(
    q_short,
    k_short,
    v_short,
    dout_short,
    doc_lengths,
    doc_dest,
    q_long,
    k_long,
    v_long,
    dout_long,
    block_order,
):
    ways = lax.axis_size("ctx")
    ranks = lax.axis_size("dp")
    steps = peer_order(ways)
    heads_each = q_long.shape[2] // HEAD_DIM // ways
    arrays = (q_long, k_long, v_long, dout_long)

    def swap(value, step):
        return lax.ppermute(value, "ctx", [(i, i ^ step) for i in range(ways)])

    far = [step for step in steps if step != 1]
    first = [(0, step) for step in far]
    later = [(0, 1), (0, 0)] + [(head, step) for head in range(1, heads_each) for step in steps + [0]]
    packed = dict(zip(first, pack(first, ways, arrays)))
    packed.update(zip(later, pack(later, ways, arrays, (packed[first[0]],))))
    arrived = [[swap(packed[head, step], step) for step in steps] + [packed[head, 0]] for head in range(heads_each)]
    shorts = (q_short, k_short, v_short, dout_short)
    short_heads = q_short.shape[1] // HEAD_DIM
    short = short_attention(0, short_heads, doc_lengths, doc_dest, shorts, None, None, block_order)
    (tail, table), short = short[4:], short[:4]
    received = lax.ppermute(tail, "dp", [(i, (i + ranks // 2) % ranks) for i in range(ranks)])
    pieces = []
    for head in range(heads_each):
        made = long_attention(ways, table, arrived[head], (pieces[-1][-1] if head else tail,))
        pieces.append([swap(value, step) for value, step in zip(made[: ways - 1], steps)] + [made[-1]])
    for head in range(1, short_heads):
        short = short_attention(head, short_heads, doc_lengths, doc_dest, shorts, short, pieces[-1][-1])
    whole = {(head, step): pieces[head][index] for head in range(heads_each) for index, step in enumerate(steps + [0])}
    final = [(heads_each - 1, step) for step in far]
    sooner = [key for key in whole if key not in final]
    outs = join(sooner, ways, [whole[key] for key in sooner], None, q_long.shape, received, short[0])
    out_short = outs[4]
    outs = join(final, ways, [whole[key] for key in final], outs[:4], q_long.shape)
    out_long, dq_long, dk_long, dv_long = outs
    dq_short, dk_short, dv_short = short[1:]
    return (out_short, dq_short, dk_short, dv_short, out_long, dq_long, dk_long, dv_long)


def solution(mesh):
    flat = P("dp", "ctx")
    deep = P("dp", "ctx", None)

    return jax.shard_map(
        shards,
        mesh=mesh,
        in_specs=(flat,) * 4 + (P(), P()) + (deep,) * 4 + (P(),),
        out_specs=(flat,) * 4 + (deep,) * 4,
        check_vma=False,
    )
```

```python
import functools

import jax
import jax.numpy as jnp
from jax import lax
from jax.experimental import pallas as pl
from jax.experimental.pallas import tpu as pltpu
from jax.sharding import PartitionSpec as P


HEAD_DIM = 128
NEG = -1e30
LOG2E = 1.4426950408889634


def dot_rows(left, right):
    return lax.dot_general(
        left, right, (((1,), (1,)), ((), ())), preferred_element_type=jnp.float32
    )


def dot(left, right):
    return jnp.dot(left, right, preferred_element_type=jnp.float32)


def score_stage(queries, douts, keys, values):
    return dot_rows(keys, queries), dot_rows(values, douts)


def softmax_stage(scores, dprobs, tile, columns, mask_tile, scale):
    key_tiles = scores.shape[0] // tile
    weight_cols = []
    grad_cols = []
    for b, (first, last) in enumerate(columns):
        lanes = slice(b * tile, (b + 1) * tile)
        s_tiles = []
        top = None
        for j in range(first, last):
            s = mask_tile(scores[j * tile : (j + 1) * tile, lanes], j, b)
            s_tiles.append(s)
            part = jnp.max(s, axis=0, keepdims=True)
            top = part if top is None else jnp.maximum(top, part)
        e_tiles = [jnp.exp2((s - top) * (scale * LOG2E)) for s in s_tiles]
        total = sum(jnp.sum(e, axis=0, keepdims=True) for e in e_tiles)
        inverse = 1.0 / total
        p_tiles = [e * inverse for e in e_tiles]
        d_tiles = [dprobs[j * tile : (j + 1) * tile, lanes] for j in range(first, last)]
        delta = sum(jnp.sum(p * d, axis=0, keepdims=True) for p, d in zip(p_tiles, d_tiles))
        w_tiles = [p.astype(jnp.bfloat16) for p in p_tiles]
        g_tiles = [(p * (d - delta)).astype(jnp.bfloat16) for p, d in zip(p_tiles, d_tiles)]
        zero = jnp.zeros((tile, tile), jnp.bfloat16)
        before = [zero] * first
        after = [zero] * (key_tiles - last)
        weight_cols.append(jnp.concatenate(before + w_tiles + after, axis=0))
        grad_cols.append(jnp.concatenate(before + g_tiles + after, axis=0))
    return jnp.concatenate(weight_cols, axis=1), jnp.concatenate(grad_cols, axis=1)


def product_stage(weights, grads, queries, douts, keys_t, values_t, scale):
    attended = dot(values_t, weights).astype(jnp.bfloat16).T
    grad_q = (dot(keys_t, grads) * scale).astype(jnp.bfloat16).T
    return attended, grad_q, dot(grads, queries), dot(weights, douts)


def staged(blocks, scores_of, softmax_of, products_of, ahead=1):
    scores = {}
    for step in range(blocks + ahead):
        if step < blocks:
            scores[step] = scores_of(step)
        if step >= ahead:
            block = step - ahead
            products_of(block, *softmax_of(block, *scores.pop(block)))


def causal(s, tile):
    key = lax.broadcasted_iota(jnp.int32, (tile, tile), 0)
    query = lax.broadcasted_iota(jnp.int32, (tile, tile), 1)
    return jnp.where(key <= query, s, NEG)


def short_kernel(head, heads, lengths, dests, q_hbm, k_hbm, v_hbm, d_hbm, *rest):
    if head > 0:
        rest = rest[5:]
    else:
        order, rest = rest[0], rest[1:]
    out_hbm, dq_hbm, dk_hbm, dv_hbm = rest[:4]
    rest = rest[4:]
    if head == 0:
        (tail_ref, table_ref), rest = rest[:2], rest[2:]
        for index in range(order.shape[0]):
            table_ref[index : index + 1, :] = jnp.full((1, table_ref.shape[1]), order[index], jnp.int32)
    held, made, in_sem, out_sem = rest[:4]
    scale = HEAD_DIM ** (-0.5)
    tokens = q_hbm.shape[0]
    tile = tokens // 6
    span = 2 * tile
    rank = lax.axis_index("dp")
    count = lengths.shape[1]
    column = pl.ds(head * HEAD_DIM, HEAD_DIM)

    loads = [
        pltpu.make_async_copy(ref.at[:, column], held.at[slot], in_sem)
        for slot, ref in enumerate((q_hbm, k_hbm, v_hbm, d_hbm))
    ]
    for load in loads:
        load.start()
    others = []
    if head == 0:
        ends, end_sem = rest[4:]
        for other in range(1, heads):
            columns = pl.ds(other * HEAD_DIM, HEAD_DIM)
            for slot, ref in enumerate((q_hbm, k_hbm, v_hbm)):
                others.append(
                    pltpu.make_async_copy(
                        ref.at[pl.ds(tokens - 3 * tile, 3 * tile), columns],
                        ends.at[other - 1, slot],
                        end_sem,
                    )
                )
        for load in others:
            load.start()

    place = lax.broadcasted_iota(jnp.int32, (1, tokens), 1)
    start = jnp.zeros((1, tokens), jnp.int32)
    begin = jnp.int32(0)
    for j in range(count - 1):
        begin = begin + lengths[rank, j]
        start = jnp.where(place >= begin, begin, start)
    tail = lengths[rank, count - 1]
    moves = dests[rank, count - 1] != rank

    def store(slot, low, high, target):
        rows = pl.ds(low, high - low)
        pltpu.make_async_copy(made.at[slot, rows, :], target.at[rows, column], out_sem).start()

    pltpu.make_async_copy(held, held, in_sem).wait()
    q_ref, k_ref, v_ref, d_ref = [held.at[slot] for slot in range(4)]
    keys_t = k_ref[...].T
    values_t = v_ref[...].T
    blocks = tokens // span
    pending = {}

    def key_low(block):
        return max(0, (block - 1) * span)

    def sent(last):
        to = lax.broadcasted_iota(jnp.int32, (tile, tile), 0)
        come = lax.broadcasted_iota(jnp.int32, (tile, tile), 1)
        pick = (come == to + (tile - tail)) & moves & (to < tail)
        return dot(pick.astype(jnp.float32).astype(jnp.bfloat16), last).astype(jnp.bfloat16)

    def scores_of(block):
        low = block * span
        keys = slice(key_low(block), low + span)
        return score_stage(q_ref[low : low + span, :], d_ref[low : low + span, :], k_ref[keys, :], v_ref[keys, :])

    def softmax_of(block, scores, dprobs):
        low = block * span
        offset = (low - key_low(block)) // tile

        def mask_tile(s, j, b):
            key = lax.broadcasted_iota(jnp.int32, (tile, tile), 0)
            first = start[:, low + b * tile : low + (b + 1) * tile] - (key_low(block) + j * tile)
            allowed = key >= first
            if j == offset + b:
                query = lax.broadcasted_iota(jnp.int32, (tile, tile), 1)
                allowed = allowed & (key <= query)
            return jnp.where(allowed, s, NEG)

        columns = [(max(0, offset + b - 2), offset + b + 1) for b in range(2)]
        return softmax_stage(scores, dprobs, tile, columns, mask_tile, scale)

    def products_of(block, weights, grads):
        low = block * span
        high = low + span
        keys = slice(key_low(block), high)
        attended, grad_q, grad_k, grad_v = product_stage(
            weights,
            grads,
            q_ref[low:high, :],
            d_ref[low:high, :],
            keys_t[:, keys],
            values_t[:, keys],
            scale,
        )
        made[1, low:high, :] = grad_q
        store(1, low, high, dq_hbm)
        if high == tokens:
            last = attended[tile:, :]
            row = lax.broadcasted_iota(jnp.int32, (tile, 1), 0)
            kept = jnp.logical_not(moves & (row >= tile - tail))
            made[0, low : low + tile, :] = attended[:tile, :]
            made[0, low + tile : tokens, :] = jnp.where(kept, last, jnp.zeros_like(last))
            if head == 0:
                tail_ref[0] = sent(last)
        else:
            made[0, low:high, :] = attended
        store(0, low, high, out_hbm)
        if block > 0:
            done_k = pending["k"] + grad_k[:span]
            done_v = pending["v"] + grad_v[:span]
            made[2, low - span : low, :] = (done_k * scale).astype(jnp.bfloat16)
            made[3, low - span : low, :] = done_v.astype(jnp.bfloat16)
            store(2, low - span, low, dk_hbm)
            store(3, low - span, low, dv_hbm)
        pending["k"] = grad_k[-span:]
        pending["v"] = grad_v[-span:]
        if high == tokens:
            made[2, low:high, :] = (pending["k"] * scale).astype(jnp.bfloat16)
            made[3, low:high, :] = pending["v"].astype(jnp.bfloat16)
            store(2, low, high, dk_hbm)
            store(3, low, high, dv_hbm)

    staged(blocks, scores_of, softmax_of, products_of)
    if others:
        pltpu.make_async_copy(ends, ends, end_sem).wait()
        for other in range(1, heads):
            scores = dot_rows(ends[other - 1, 1], ends[other - 1, 0, 2 * tile :, :])
            key = lax.broadcasted_iota(jnp.int32, scores.shape, 0)
            query = lax.broadcasted_iota(jnp.int32, scores.shape, 1) + 2 * tile
            first = start[:, tokens - tile :] - (tokens - 3 * tile)
            scores = jnp.where((key >= first) & (key <= query), scores, NEG)
            grown = jnp.exp2((scores - jnp.max(scores, axis=0, keepdims=True)) * (scale * LOG2E))
            weights = (grown * (1.0 / jnp.sum(grown, axis=0, keepdims=True))).astype(jnp.bfloat16)
            tail_ref[other] = sent(dot(weights.T, ends[other - 1, 2]).astype(jnp.bfloat16))
    pltpu.make_async_copy(made, made, out_sem).wait()


def short_attention(head, heads, lengths, dests, arrays, before, after, order=None):
    tokens, width = arrays[0].shape
    move = tokens // 6
    smem = pl.BlockSpec(memory_space=pltpu.SMEM)
    hbm = pl.BlockSpec(memory_space=pltpu.HBM)
    vmem = pl.BlockSpec(memory_space=pltpu.VMEM)
    wide = jax.ShapeDtypeStruct((tokens, width), jnp.bfloat16)
    first = before is None
    extra = [order] if first else list(before[:4]) + [after]
    tile = move
    return pl.pallas_call(
        functools.partial(short_kernel, head, heads),
        in_specs=[smem] * 2 + [hbm] * 4 + ([smem] if first else [hbm] * 4 + [pl.BlockSpec(memory_space=pl.ANY)]),
        out_specs=[hbm] * 4 + ([vmem] * 2 if first else []),
        out_shape=[jax.ShapeDtypeStruct((tokens + move, width), jnp.bfloat16), wide, wide, wide]
        + (
            [
                jax.ShapeDtypeStruct((heads, move, HEAD_DIM), jnp.bfloat16),
                jax.ShapeDtypeStruct((order.shape[0], HEAD_DIM), jnp.int32),
            ]
            if first
            else []
        ),
        scratch_shapes=[
            pltpu.VMEM((4, tokens, HEAD_DIM), jnp.bfloat16),
            pltpu.VMEM((4, tokens, HEAD_DIM), jnp.bfloat16),
            pltpu.SemaphoreType.DMA,
            pltpu.SemaphoreType.DMA,
        ]
        + (
            [
                pltpu.VMEM((max(heads - 1, 1), 3, 3 * tile, HEAD_DIM), jnp.bfloat16),
                pltpu.SemaphoreType.DMA,
            ]
            if first
            else []
        ),
        input_output_aliases={} if first else {6 + i: i for i in range(4)},
        compiler_params=pltpu.CompilerParams(vmem_limit_bytes=16 << 20),
        cost_estimate=pl.CostEstimate(flops=10**9, bytes_accessed=3 * 10**6, transcendentals=0),
    )(lengths, dests, *arrays, *extra)


def peer_order(ways):
    return [step for step in range(2, ways)] + [1]


def pack_kernel(parts, ways, after, q_ref, k_ref, v_ref, d_ref, *rest):
    rest = rest[after:]
    outs, (all_bytes, sem) = rest[: len(parts)], rest[len(parts) :]
    own = lax.axis_index("ctx")
    per = q_ref.shape[2] // ways
    for out, (head, step) in zip(outs, parts):
        column = pl.multiple_of((own ^ step) * per + head * HEAD_DIM, HEAD_DIM)
        for slot, ref in enumerate((q_ref, k_ref, v_ref, d_ref)):
            pltpu.make_async_copy(ref.at[0, :, pl.ds(column, HEAD_DIM)], out.at[slot], sem).start()
    pltpu.make_async_copy(all_bytes, all_bytes, sem).wait()


def pack(parts, ways, arrays, after=()):
    rows = arrays[0].shape[1]
    return pl.pallas_call(
        functools.partial(pack_kernel, parts, ways, len(after)),
        in_specs=[pl.BlockSpec(memory_space=pltpu.HBM)] * 4 + [pl.BlockSpec(memory_space=pl.ANY)] * len(after),
        out_specs=[pl.BlockSpec(memory_space=pltpu.VMEM)] * len(parts),
        out_shape=[jax.ShapeDtypeStruct((4, rows, HEAD_DIM), jnp.bfloat16)] * len(parts),
        scratch_shapes=[
            pltpu.VMEM((4 * len(parts), rows, HEAD_DIM), jnp.bfloat16),
            pltpu.SemaphoreType.DMA,
        ],
        compiler_params=pltpu.CompilerParams(vmem_limit_bytes=8 << 20),
        cost_estimate=pl.CostEstimate(flops=0, bytes_accessed=2 * 10**6, transcendentals=0),
    )(*[pltpu.with_memory_space_constraint(array, pltpu.HBM) for array in arrays], *after)


def long_kernel(ways, linked, order, *rest):
    rest = rest[linked:]
    steps = peer_order(ways) + [0]
    arrived = rest[:ways]
    outs = rest[ways : 2 * ways]
    held, made = rest[2 * ways :]
    scale = HEAD_DIM ** (-0.5)
    own = lax.axis_index("ctx")
    rows = arrived[0].shape[1]
    half = rows // 2
    total = rows * ways

    def spot(device, part):
        return pl.ds(pl.multiple_of(order[device * 2 + part, 0] * half, half), half)

    for buffer, step in zip(arrived, steps):
        for part in range(2):
            piece = slice(part * half, (part + 1) * half)
            for slot in range(4):
                held[slot, spot(own ^ step, part), :] = buffer[slot, piece, :]

    tile = HEAD_DIM
    span = 2 * tile
    blocks = total // span
    keys_t = held[1].T
    values_t = held[2].T
    sum_k = [None] * blocks
    sum_v = [None] * blocks

    def scores_of(block):
        low, high = block * span, (block + 1) * span
        return score_stage(held[0, low:high, :], held[3, low:high, :], held[1, :high, :], held[2, :high, :])

    def softmax_of(block, scores, dprobs):
        first = block * span // tile

        def mask_tile(s, j, b):
            return causal(s, tile) if j == first + b else s

        columns = [(0, first + b + 1) for b in range(span // tile)]
        return softmax_stage(scores, dprobs, tile, columns, mask_tile, scale)

    def products_of(block, weights, grads):
        low, high = block * span, (block + 1) * span
        attended, grad_q, grad_k, grad_v = product_stage(
            weights, grads, held[0, low:high, :], held[3, low:high, :], keys_t[:, :high], values_t[:, :high], scale
        )
        made[0, low:high, :] = attended
        made[1, low:high, :] = grad_q
        for part in range(block + 1):
            piece = slice(part * span, (part + 1) * span)
            sum_k[part] = grad_k[piece] if sum_k[part] is None else sum_k[part] + grad_k[piece]
            sum_v[part] = grad_v[piece] if sum_v[part] is None else sum_v[part] + grad_v[piece]

    staged(blocks, scores_of, softmax_of, products_of)
    for part in range(blocks):
        piece = slice(part * span, (part + 1) * span)
        made[2, piece, :] = (sum_k[part] * scale).astype(jnp.bfloat16)
        made[3, piece, :] = sum_v[part].astype(jnp.bfloat16)

    for out, step in zip(outs, steps):
        for part in range(2):
            piece = slice(part * half, (part + 1) * half)
            for slot in range(4):
                out[slot, piece, :] = made[slot, spot(own ^ step, part), :]


def long_attention(ways, order, arrived, linked=()):
    anywhere = [pl.BlockSpec(memory_space=pl.ANY)] * len(linked)
    rows = arrived[0].shape[1]
    piece = jax.ShapeDtypeStruct((4, rows, HEAD_DIM), jnp.bfloat16)
    vmem = pl.BlockSpec(memory_space=pltpu.VMEM)
    return pl.pallas_call(
        functools.partial(long_kernel, ways, len(linked)),
        in_specs=[vmem] + anywhere + [vmem] * ways,
        out_specs=[vmem] * ways,
        out_shape=[piece] * ways,
        scratch_shapes=[
            pltpu.VMEM((4, rows * ways, HEAD_DIM), jnp.bfloat16),
            pltpu.VMEM((4, rows * ways, HEAD_DIM), jnp.bfloat16),
        ],
        compiler_params=pltpu.CompilerParams(vmem_limit_bytes=16 << 20),
        cost_estimate=pl.CostEstimate(flops=10**9, bytes_accessed=3 * 10**6, transcendentals=0),
    )(order, *linked, *arrived)


def join_kernel(parts, ways, olds, with_short, *refs):
    pieces = refs[: len(parts)]
    refs = refs[len(parts) :]
    if with_short:
        received, refs = refs[0], refs[1:]
    refs = refs[olds:]
    outs, refs = refs[:4], refs[4:]
    all_bytes, sem = refs[-2:]
    own = lax.axis_index("ctx")
    per = outs[0].shape[2] // ways
    for piece, (head, step) in zip(pieces, parts):
        column = pl.multiple_of((own ^ step) * per + head * HEAD_DIM, HEAD_DIM)
        for slot, out in enumerate(outs):
            pltpu.make_async_copy(piece.at[slot], out.at[0, :, pl.ds(column, HEAD_DIM)], sem).start()
    if with_short:
        short_out = refs[0]
        heads, move, _ = received.shape
        rows = pl.ds(short_out.shape[0] - move, move)
        for other in range(heads):
            columns = pl.ds(other * HEAD_DIM, HEAD_DIM)
            pltpu.make_async_copy(received.at[other], short_out.at[rows, columns], sem).start()
    pltpu.make_async_copy(all_bytes, all_bytes, sem).wait()


def join(parts, ways, pieces, outs, shape, received=None, short_out=None):
    with_short = received is not None
    vmem = pl.BlockSpec(memory_space=pltpu.VMEM)
    hbm = pl.BlockSpec(memory_space=pltpu.HBM)
    operands = list(pieces)
    in_specs = [vmem] * len(pieces)
    out_shape = [jax.ShapeDtypeStruct(shape, jnp.bfloat16)] * 4
    aliases = {}
    size = 4 * len(parts) * shape[1]
    if with_short:
        operands.append(received)
        in_specs.append(vmem)
        out_shape.append(jax.ShapeDtypeStruct(short_out.shape, jnp.bfloat16))
        size += received.shape[0] * received.shape[1]
    old = ([] if outs is None else list(outs)) + ([short_out] if with_short else [])
    first_out = 0 if outs is not None else 4
    for index, value in enumerate(old):
        aliases[len(operands)] = first_out + index
        operands.append(value)
        in_specs.append(hbm)
    return pl.pallas_call(
        functools.partial(join_kernel, parts, ways, len(old), with_short),
        in_specs=in_specs,
        out_specs=[hbm] * len(out_shape),
        out_shape=out_shape,
        scratch_shapes=[pltpu.VMEM((size, HEAD_DIM), jnp.bfloat16), pltpu.SemaphoreType.DMA],
        input_output_aliases=aliases,
        compiler_params=pltpu.CompilerParams(vmem_limit_bytes=8 << 20),
        cost_estimate=pl.CostEstimate(flops=0, bytes_accessed=10**6, transcendentals=0),
    )(*operands)


def shards(
    q_short,
    k_short,
    v_short,
    dout_short,
    doc_lengths,
    doc_dest,
    q_long,
    k_long,
    v_long,
    dout_long,
    block_order,
):
    ways = lax.axis_size("ctx")
    ranks = lax.axis_size("dp")
    steps = peer_order(ways)
    heads_each = q_long.shape[2] // HEAD_DIM // ways
    arrays = (q_long, k_long, v_long, dout_long)

    def swap(value, step):
        return lax.ppermute(value, "ctx", [(i, i ^ step) for i in range(ways)])

    far = [step for step in steps if step != 1]
    first = [(0, step) for step in far]
    later = [(0, 1), (0, 0)] + [(head, step) for head in range(1, heads_each) for step in steps + [0]]
    packed = dict(zip(first, pack(first, ways, arrays)))
    packed.update(zip(later, pack(later, ways, arrays, (packed[first[0]],))))
    arrived = [[swap(packed[head, step], step) for step in steps] + [packed[head, 0]] for head in range(heads_each)]
    shorts = (q_short, k_short, v_short, dout_short)
    short_heads = q_short.shape[1] // HEAD_DIM
    short = short_attention(0, short_heads, doc_lengths, doc_dest, shorts, None, None, block_order)
    (tail, table), short = short[4:], short[:4]
    received = lax.ppermute(tail, "dp", [(i, (i + ranks // 2) % ranks) for i in range(ranks)])
    pieces = []
    for head in range(heads_each):
        made = long_attention(ways, table, arrived[head], (pieces[-1][-1] if head else tail,))
        pieces.append([swap(value, step) for value, step in zip(made[: ways - 1], steps)] + [made[-1]])
    for head in range(1, short_heads):
        short = short_attention(head, short_heads, doc_lengths, doc_dest, shorts, short, pieces[-1][-1])
    whole = {(head, step): pieces[head][index] for head in range(heads_each) for index, step in enumerate(steps + [0])}
    final = [(heads_each - 1, step) for step in far]
    sooner = [key for key in whole if key not in final]
    outs = join(sooner, ways, [whole[key] for key in sooner], None, q_long.shape)
    outs = join(final, ways, [whole[key] for key in final], outs[:4], q_long.shape, received, short[0])
    out_long, dq_long, dk_long, dv_long, out_short = outs
    dq_short, dk_short, dv_short = short[1:]
    return (out_short, dq_short, dk_short, dv_short, out_long, dq_long, dk_long, dv_long)


def solution(mesh):
    flat = P("dp", "ctx")
    deep = P("dp", "ctx", None)

    return jax.shard_map(
        shards,
        mesh=mesh,
        in_specs=(flat,) * 4 + (P(), P()) + (deep,) * 4 + (P(),),
        out_specs=(flat,) * 4 + (deep,) * 4,
        check_vma=False,
    )
```

```python
import functools

import jax
import jax.numpy as jnp
from jax import lax
from jax.experimental import pallas as pl
from jax.experimental.pallas import tpu as pltpu
from jax.sharding import PartitionSpec as P


HEAD_DIM = 128
NEG = -1e30
LOG2E = 1.4426950408889634


def dot_rows(left, right):
    return lax.dot_general(
        left, right, (((1,), (1,)), ((), ())), preferred_element_type=jnp.float32
    )


def dot(left, right):
    return jnp.dot(left, right, preferred_element_type=jnp.float32)


def score_stage(queries, douts, keys, values):
    return dot_rows(keys, queries), dot_rows(values, douts)


def softmax_stage(scores, dprobs, values_t, douts_t, tile, columns, mask_tile, scale):
    key_tiles = scores.shape[0] // tile
    zero = jnp.zeros((tile, tile), jnp.bfloat16)

    def column(tiles, first, last):
        return jnp.concatenate([zero] * first + tiles + [zero] * (key_tiles - last), axis=0)

    probs = []
    weight_cols = []
    for b, (first, last) in enumerate(columns):
        lanes = slice(b * tile, (b + 1) * tile)
        s_tiles = []
        top = None
        for j in range(first, last):
            s = mask_tile(scores[j * tile : (j + 1) * tile, lanes], j, b)
            s_tiles.append(s)
            part = jnp.max(s, axis=0, keepdims=True)
            top = part if top is None else jnp.maximum(top, part)
        e_tiles = [jnp.exp2((s - top) * (scale * LOG2E)) for s in s_tiles]
        total = sum(jnp.sum(e, axis=0, keepdims=True) for e in e_tiles)
        inverse = 1.0 / total
        p_tiles = [e * inverse for e in e_tiles]
        probs.append(p_tiles)
        weight_cols.append(column([p.astype(jnp.bfloat16) for p in p_tiles], first, last))
    weights = jnp.concatenate(weight_cols, axis=1)
    attended_t = dot(values_t, weights).astype(jnp.bfloat16)
    delta = jnp.sum(attended_t.astype(jnp.float32) * douts_t.astype(jnp.float32), axis=0, keepdims=True)
    grad_cols = []
    for b, (first, last) in enumerate(columns):
        lanes = slice(b * tile, (b + 1) * tile)
        g_tiles = [
            (p * (dprobs[j * tile : (j + 1) * tile, lanes] - delta[:, lanes])).astype(jnp.bfloat16)
            for j, p in zip(range(first, last), probs[b])
        ]
        grad_cols.append(column(g_tiles, first, last))
    return weights, jnp.concatenate(grad_cols, axis=1), attended_t


def product_stage(weights, grads, attended_t, queries, douts, keys_t, scale):
    grad_q = (dot(keys_t, grads) * scale).astype(jnp.bfloat16).T
    return attended_t.T, grad_q, dot(grads, queries), dot(weights, douts)


def staged(blocks, scores_of, softmax_of, products_of, ahead=1):
    scores = {}
    for step in range(blocks + ahead):
        if step < blocks:
            scores[step] = scores_of(step)
        if step >= ahead:
            block = step - ahead
            products_of(block, *softmax_of(block, *scores.pop(block)))


def causal(s, tile):
    key = lax.broadcasted_iota(jnp.int32, (tile, tile), 0)
    query = lax.broadcasted_iota(jnp.int32, (tile, tile), 1)
    return jnp.where(key <= query, s, NEG)


def short_kernel(head, heads, lengths, dests, q_hbm, k_hbm, v_hbm, d_hbm, *rest):
    if head > 0:
        rest = rest[5:]
    else:
        order, rest = rest[0], rest[1:]
    out_hbm, dq_hbm, dk_hbm, dv_hbm = rest[:4]
    rest = rest[4:]
    if head == 0:
        (tail_ref, table_ref), rest = rest[:2], rest[2:]
        for index in range(order.shape[0]):
            table_ref[index : index + 1, :] = jnp.full((1, table_ref.shape[1]), order[index], jnp.int32)
    held, made, in_sem, out_sem = rest[:4]
    scale = HEAD_DIM ** (-0.5)
    tokens = q_hbm.shape[0]
    tile = tokens // 6
    span = 2 * tile
    rank = lax.axis_index("dp")
    count = lengths.shape[1]
    column = pl.ds(head * HEAD_DIM, HEAD_DIM)

    loads = [
        pltpu.make_async_copy(ref.at[:, column], held.at[slot], in_sem)
        for slot, ref in enumerate((q_hbm, k_hbm, v_hbm, d_hbm))
    ]
    for load in loads:
        load.start()
    others = []
    if head == 0:
        ends, end_sem = rest[4:]
        for other in range(1, heads):
            columns = pl.ds(other * HEAD_DIM, HEAD_DIM)
            for slot, ref in enumerate((q_hbm, k_hbm, v_hbm)):
                others.append(
                    pltpu.make_async_copy(
                        ref.at[pl.ds(tokens - 3 * tile, 3 * tile), columns],
                        ends.at[other - 1, slot],
                        end_sem,
                    )
                )
        for load in others:
            load.start()

    place = lax.broadcasted_iota(jnp.int32, (1, tokens), 1)
    start = jnp.zeros((1, tokens), jnp.int32)
    begin = jnp.int32(0)
    for j in range(count - 1):
        begin = begin + lengths[rank, j]
        start = jnp.where(place >= begin, begin, start)
    tail = lengths[rank, count - 1]
    moves = dests[rank, count - 1] != rank

    def store(slot, low, high, target):
        rows = pl.ds(low, high - low)
        pltpu.make_async_copy(made.at[slot, rows, :], target.at[rows, column], out_sem).start()

    pltpu.make_async_copy(held, held, in_sem).wait()
    q_ref, k_ref, v_ref, d_ref = [held.at[slot] for slot in range(4)]
    keys_t = k_ref[...].T
    values_t = v_ref[...].T
    douts_t = d_ref[...].T
    blocks = tokens // span
    pending = {}

    def key_low(block):
        return max(0, (block - 1) * span)

    def sent(last):
        to = lax.broadcasted_iota(jnp.int32, (tile, tile), 0)
        come = lax.broadcasted_iota(jnp.int32, (tile, tile), 1)
        pick = (come == to + (tile - tail)) & moves & (to < tail)
        return dot(pick.astype(jnp.float32).astype(jnp.bfloat16), last).astype(jnp.bfloat16)

    def scores_of(block):
        low = block * span
        keys = slice(key_low(block), low + span)
        return score_stage(q_ref[low : low + span, :], d_ref[low : low + span, :], k_ref[keys, :], v_ref[keys, :])

    def softmax_of(block, scores, dprobs):
        low = block * span
        offset = (low - key_low(block)) // tile

        def mask_tile(s, j, b):
            key = lax.broadcasted_iota(jnp.int32, (tile, tile), 0)
            first = start[:, low + b * tile : low + (b + 1) * tile] - (key_low(block) + j * tile)
            allowed = key >= first
            if j == offset + b:
                query = lax.broadcasted_iota(jnp.int32, (tile, tile), 1)
                allowed = allowed & (key <= query)
            return jnp.where(allowed, s, NEG)

        columns = [(max(0, offset + b - 2), offset + b + 1) for b in range(2)]
        keys = slice(key_low(block), low + span)
        return softmax_stage(
            scores, dprobs, values_t[:, keys], douts_t[:, low : low + span], tile, columns, mask_tile, scale
        )

    def products_of(block, weights, grads, attended_t):
        low = block * span
        high = low + span
        keys = slice(key_low(block), high)
        attended, grad_q, grad_k, grad_v = product_stage(
            weights,
            grads,
            attended_t,
            q_ref[low:high, :],
            d_ref[low:high, :],
            keys_t[:, keys],
            scale,
        )
        made[1, low:high, :] = grad_q
        store(1, low, high, dq_hbm)
        if high == tokens:
            last = attended[tile:, :]
            row = lax.broadcasted_iota(jnp.int32, (tile, 1), 0)
            kept = jnp.logical_not(moves & (row >= tile - tail))
            made[0, low : low + tile, :] = attended[:tile, :]
            made[0, low + tile : tokens, :] = jnp.where(kept, last, jnp.zeros_like(last))
            if head == 0:
                tail_ref[0] = sent(last)
        else:
            made[0, low:high, :] = attended
        store(0, low, high, out_hbm)
        if block > 0:
            done_k = pending["k"] + grad_k[:span]
            done_v = pending["v"] + grad_v[:span]
            made[2, low - span : low, :] = (done_k * scale).astype(jnp.bfloat16)
            made[3, low - span : low, :] = done_v.astype(jnp.bfloat16)
            store(2, low - span, low, dk_hbm)
            store(3, low - span, low, dv_hbm)
        pending["k"] = grad_k[-span:]
        pending["v"] = grad_v[-span:]
        if high == tokens:
            made[2, low:high, :] = (pending["k"] * scale).astype(jnp.bfloat16)
            made[3, low:high, :] = pending["v"].astype(jnp.bfloat16)
            store(2, low, high, dk_hbm)
            store(3, low, high, dv_hbm)

    staged(blocks, scores_of, softmax_of, products_of)
    if others:
        pltpu.make_async_copy(ends, ends, end_sem).wait()
        for other in range(1, heads):
            scores = dot_rows(ends[other - 1, 1], ends[other - 1, 0, 2 * tile :, :])
            key = lax.broadcasted_iota(jnp.int32, scores.shape, 0)
            query = lax.broadcasted_iota(jnp.int32, scores.shape, 1) + 2 * tile
            first = start[:, tokens - tile :] - (tokens - 3 * tile)
            scores = jnp.where((key >= first) & (key <= query), scores, NEG)
            grown = jnp.exp2((scores - jnp.max(scores, axis=0, keepdims=True)) * (scale * LOG2E))
            weights = (grown * (1.0 / jnp.sum(grown, axis=0, keepdims=True))).astype(jnp.bfloat16)
            tail_ref[other] = sent(dot(weights.T, ends[other - 1, 2]).astype(jnp.bfloat16))
    pltpu.make_async_copy(made, made, out_sem).wait()


def short_attention(head, heads, lengths, dests, arrays, before, after, order=None):
    tokens, width = arrays[0].shape
    move = tokens // 6
    smem = pl.BlockSpec(memory_space=pltpu.SMEM)
    hbm = pl.BlockSpec(memory_space=pltpu.HBM)
    vmem = pl.BlockSpec(memory_space=pltpu.VMEM)
    wide = jax.ShapeDtypeStruct((tokens, width), jnp.bfloat16)
    first = before is None
    extra = [order] if first else list(before[:4]) + [after]
    tile = move
    return pl.pallas_call(
        functools.partial(short_kernel, head, heads),
        in_specs=[smem] * 2 + [hbm] * 4 + ([smem] if first else [hbm] * 4 + [pl.BlockSpec(memory_space=pl.ANY)]),
        out_specs=[hbm] * 4 + ([vmem] * 2 if first else []),
        out_shape=[jax.ShapeDtypeStruct((tokens + move, width), jnp.bfloat16), wide, wide, wide]
        + (
            [
                jax.ShapeDtypeStruct((heads, move, HEAD_DIM), jnp.bfloat16),
                jax.ShapeDtypeStruct((order.shape[0], HEAD_DIM), jnp.int32),
            ]
            if first
            else []
        ),
        scratch_shapes=[
            pltpu.VMEM((4, tokens, HEAD_DIM), jnp.bfloat16),
            pltpu.VMEM((4, tokens, HEAD_DIM), jnp.bfloat16),
            pltpu.SemaphoreType.DMA,
            pltpu.SemaphoreType.DMA,
        ]
        + (
            [
                pltpu.VMEM((max(heads - 1, 1), 3, 3 * tile, HEAD_DIM), jnp.bfloat16),
                pltpu.SemaphoreType.DMA,
            ]
            if first
            else []
        ),
        input_output_aliases={} if first else {6 + i: i for i in range(4)},
        compiler_params=pltpu.CompilerParams(vmem_limit_bytes=16 << 20),
        cost_estimate=pl.CostEstimate(flops=10**9, bytes_accessed=3 * 10**6, transcendentals=0),
    )(lengths, dests, *arrays, *extra)


def peer_order(ways):
    return [step for step in range(2, ways)] + [1]


def pack_kernel(parts, ways, after, q_ref, k_ref, v_ref, d_ref, *rest):
    rest = rest[after:]
    outs, (all_bytes, sem) = rest[: len(parts)], rest[len(parts) :]
    own = lax.axis_index("ctx")
    per = q_ref.shape[2] // ways
    for out, (head, step) in zip(outs, parts):
        column = pl.multiple_of((own ^ step) * per + head * HEAD_DIM, HEAD_DIM)
        for slot, ref in enumerate((q_ref, k_ref, v_ref, d_ref)):
            pltpu.make_async_copy(ref.at[0, :, pl.ds(column, HEAD_DIM)], out.at[slot], sem).start()
    pltpu.make_async_copy(all_bytes, all_bytes, sem).wait()


def pack(parts, ways, arrays, after=()):
    rows = arrays[0].shape[1]
    return pl.pallas_call(
        functools.partial(pack_kernel, parts, ways, len(after)),
        in_specs=[pl.BlockSpec(memory_space=pltpu.HBM)] * 4 + [pl.BlockSpec(memory_space=pl.ANY)] * len(after),
        out_specs=[pl.BlockSpec(memory_space=pltpu.VMEM)] * len(parts),
        out_shape=[jax.ShapeDtypeStruct((4, rows, HEAD_DIM), jnp.bfloat16)] * len(parts),
        scratch_shapes=[
            pltpu.VMEM((4 * len(parts), rows, HEAD_DIM), jnp.bfloat16),
            pltpu.SemaphoreType.DMA,
        ],
        compiler_params=pltpu.CompilerParams(vmem_limit_bytes=8 << 20),
        cost_estimate=pl.CostEstimate(flops=0, bytes_accessed=2 * 10**6, transcendentals=0),
    )(*[pltpu.with_memory_space_constraint(array, pltpu.HBM) for array in arrays], *after)


def long_kernel(ways, linked, order, *rest):
    rest = rest[linked:]
    steps = peer_order(ways) + [0]
    arrived = rest[:ways]
    outs = rest[ways : 2 * ways]
    held, made = rest[2 * ways :]
    scale = HEAD_DIM ** (-0.5)
    own = lax.axis_index("ctx")
    rows = arrived[0].shape[1]
    half = rows // 2
    total = rows * ways

    def spot(device, part):
        return pl.ds(pl.multiple_of(order[device * 2 + part, 0] * half, half), half)

    for buffer, step in zip(arrived, steps):
        for part in range(2):
            piece = slice(part * half, (part + 1) * half)
            for slot in range(4):
                held[slot, spot(own ^ step, part), :] = buffer[slot, piece, :]

    tile = HEAD_DIM
    span = 2 * tile
    blocks = total // span
    keys_t = held[1].T
    values_t = held[2].T
    douts_t = held[3].T
    sum_k = [None] * blocks
    sum_v = [None] * blocks

    def scores_of(block):
        low, high = block * span, (block + 1) * span
        return score_stage(held[0, low:high, :], held[3, low:high, :], held[1, :high, :], held[2, :high, :])

    def softmax_of(block, scores, dprobs):
        first = block * span // tile

        def mask_tile(s, j, b):
            return causal(s, tile) if j == first + b else s

        columns = [(0, first + b + 1) for b in range(span // tile)]
        low, high = block * span, (block + 1) * span
        return softmax_stage(
            scores, dprobs, values_t[:, :high], douts_t[:, low:high], tile, columns, mask_tile, scale
        )

    def products_of(block, weights, grads, attended_t):
        low, high = block * span, (block + 1) * span
        attended, grad_q, grad_k, grad_v = product_stage(
            weights, grads, attended_t, held[0, low:high, :], held[3, low:high, :], keys_t[:, :high], scale
        )
        made[0, low:high, :] = attended
        made[1, low:high, :] = grad_q
        for part in range(block + 1):
            piece = slice(part * span, (part + 1) * span)
            sum_k[part] = grad_k[piece] if sum_k[part] is None else sum_k[part] + grad_k[piece]
            sum_v[part] = grad_v[piece] if sum_v[part] is None else sum_v[part] + grad_v[piece]

    staged(blocks, scores_of, softmax_of, products_of)
    for part in range(blocks):
        piece = slice(part * span, (part + 1) * span)
        made[2, piece, :] = (sum_k[part] * scale).astype(jnp.bfloat16)
        made[3, piece, :] = sum_v[part].astype(jnp.bfloat16)

    for out, step in zip(outs, steps):
        for part in range(2):
            piece = slice(part * half, (part + 1) * half)
            for slot in range(4):
                out[slot, piece, :] = made[slot, spot(own ^ step, part), :]


def long_attention(ways, order, arrived, linked=()):
    anywhere = [pl.BlockSpec(memory_space=pl.ANY)] * len(linked)
    rows = arrived[0].shape[1]
    piece = jax.ShapeDtypeStruct((4, rows, HEAD_DIM), jnp.bfloat16)
    vmem = pl.BlockSpec(memory_space=pltpu.VMEM)
    return pl.pallas_call(
        functools.partial(long_kernel, ways, len(linked)),
        in_specs=[vmem] + anywhere + [vmem] * ways,
        out_specs=[vmem] * ways,
        out_shape=[piece] * ways,
        scratch_shapes=[
            pltpu.VMEM((4, rows * ways, HEAD_DIM), jnp.bfloat16),
            pltpu.VMEM((4, rows * ways, HEAD_DIM), jnp.bfloat16),
        ],
        compiler_params=pltpu.CompilerParams(vmem_limit_bytes=16 << 20),
        cost_estimate=pl.CostEstimate(flops=10**9, bytes_accessed=3 * 10**6, transcendentals=0),
    )(order, *linked, *arrived)


def join_kernel(parts, ways, olds, with_short, *refs):
    pieces = refs[: len(parts)]
    refs = refs[len(parts) :]
    if with_short:
        received, refs = refs[0], refs[1:]
    refs = refs[olds:]
    outs, refs = refs[:4], refs[4:]
    all_bytes, sem = refs[-2:]
    own = lax.axis_index("ctx")
    per = outs[0].shape[2] // ways
    for piece, (head, step) in zip(pieces, parts):
        column = pl.multiple_of((own ^ step) * per + head * HEAD_DIM, HEAD_DIM)
        for slot, out in enumerate(outs):
            pltpu.make_async_copy(piece.at[slot], out.at[0, :, pl.ds(column, HEAD_DIM)], sem).start()
    if with_short:
        short_out = refs[0]
        heads, move, _ = received.shape
        rows = pl.ds(short_out.shape[0] - move, move)
        for other in range(heads):
            columns = pl.ds(other * HEAD_DIM, HEAD_DIM)
            pltpu.make_async_copy(received.at[other], short_out.at[rows, columns], sem).start()
    pltpu.make_async_copy(all_bytes, all_bytes, sem).wait()


def join(parts, ways, pieces, outs, shape, received=None, short_out=None):
    with_short = received is not None
    vmem = pl.BlockSpec(memory_space=pltpu.VMEM)
    hbm = pl.BlockSpec(memory_space=pltpu.HBM)
    operands = list(pieces)
    in_specs = [vmem] * len(pieces)
    out_shape = [jax.ShapeDtypeStruct(shape, jnp.bfloat16)] * 4
    aliases = {}
    size = 4 * len(parts) * shape[1]
    if with_short:
        operands.append(received)
        in_specs.append(vmem)
        out_shape.append(jax.ShapeDtypeStruct(short_out.shape, jnp.bfloat16))
        size += received.shape[0] * received.shape[1]
    old = ([] if outs is None else list(outs)) + ([short_out] if with_short else [])
    first_out = 0 if outs is not None else 4
    for index, value in enumerate(old):
        aliases[len(operands)] = first_out + index
        operands.append(value)
        in_specs.append(hbm)
    return pl.pallas_call(
        functools.partial(join_kernel, parts, ways, len(old), with_short),
        in_specs=in_specs,
        out_specs=[hbm] * len(out_shape),
        out_shape=out_shape,
        scratch_shapes=[pltpu.VMEM((size, HEAD_DIM), jnp.bfloat16), pltpu.SemaphoreType.DMA],
        input_output_aliases=aliases,
        compiler_params=pltpu.CompilerParams(vmem_limit_bytes=8 << 20),
        cost_estimate=pl.CostEstimate(flops=0, bytes_accessed=10**6, transcendentals=0),
    )(*operands)


def shards(
    q_short,
    k_short,
    v_short,
    dout_short,
    doc_lengths,
    doc_dest,
    q_long,
    k_long,
    v_long,
    dout_long,
    block_order,
):
    ways = lax.axis_size("ctx")
    ranks = lax.axis_size("dp")
    steps = peer_order(ways)
    heads_each = q_long.shape[2] // HEAD_DIM // ways
    arrays = (q_long, k_long, v_long, dout_long)

    def swap(value, step):
        return lax.ppermute(value, "ctx", [(i, i ^ step) for i in range(ways)])

    far = [step for step in steps if step != 1]
    first = [(0, step) for step in far]
    later = [(0, 1), (0, 0)] + [(head, step) for head in range(1, heads_each) for step in steps + [0]]
    packed = dict(zip(first, pack(first, ways, arrays)))
    packed.update(zip(later, pack(later, ways, arrays, (packed[first[0]],))))
    arrived = [[swap(packed[head, step], step) for step in steps] + [packed[head, 0]] for head in range(heads_each)]
    shorts = (q_short, k_short, v_short, dout_short)
    short_heads = q_short.shape[1] // HEAD_DIM
    short = short_attention(0, short_heads, doc_lengths, doc_dest, shorts, None, None, block_order)
    (tail, table), short = short[4:], short[:4]
    received = lax.ppermute(tail, "dp", [(i, (i + ranks // 2) % ranks) for i in range(ranks)])
    pieces = []
    for head in range(heads_each):
        made = long_attention(ways, table, arrived[head], (pieces[-1][-1] if head else tail,))
        pieces.append([swap(value, step) for value, step in zip(made[: ways - 1], steps)] + [made[-1]])
    for head in range(1, short_heads):
        short = short_attention(head, short_heads, doc_lengths, doc_dest, shorts, short, pieces[-1][-1])
    whole = {(head, step): pieces[head][index] for head in range(heads_each) for index, step in enumerate(steps + [0])}
    final = [(heads_each - 1, step) for step in far]
    sooner = [key for key in whole if key not in final]
    outs = join(sooner, ways, [whole[key] for key in sooner], None, q_long.shape)
    outs = join(final, ways, [whole[key] for key in final], outs[:4], q_long.shape, received, short[0])
    out_long, dq_long, dk_long, dv_long, out_short = outs
    dq_short, dk_short, dv_short = short[1:]
    return (out_short, dq_short, dk_short, dv_short, out_long, dq_long, dk_long, dv_long)


def solution(mesh):
    flat = P("dp", "ctx")
    deep = P("dp", "ctx", None)

    return jax.shard_map(
        shards,
        mesh=mesh,
        in_specs=(flat,) * 4 + (P(), P()) + (deep,) * 4 + (P(),),
        out_specs=(flat,) * 4 + (deep,) * 4,
        check_vma=False,
    )
```

```python
import functools

import jax
import jax.numpy as jnp
from jax import lax
from jax.experimental import pallas as pl
from jax.experimental.pallas import tpu as pltpu
from jax.sharding import PartitionSpec as P


HEAD_DIM = 128
NEG = -1e30
LOG2E = 1.4426950408889634


def dot_rows(left, right):
    return lax.dot_general(
        left, right, (((1,), (1,)), ((), ())), preferred_element_type=jnp.float32
    )


def dot(left, right):
    return jnp.dot(left, right, preferred_element_type=jnp.float32)


def score_stage(queries, douts, keys, values):
    return dot_rows(keys, queries), dot_rows(values, douts)


def softmax_stage(scores, dprobs, values_t, douts_t, tile, columns, mask_tile, scale):
    key_tiles = scores.shape[0] // tile
    zero = jnp.zeros((tile, tile), jnp.bfloat16)

    def column(tiles, first, last):
        return jnp.concatenate([zero] * first + tiles + [zero] * (key_tiles - last), axis=0)

    probs = []
    weight_cols = []
    for b, (first, last) in enumerate(columns):
        lanes = slice(b * tile, (b + 1) * tile)
        s_tiles = []
        top = None
        for j in range(first, last):
            s = mask_tile(scores[j * tile : (j + 1) * tile, lanes], j, b)
            s_tiles.append(s)
            part = jnp.max(s, axis=0, keepdims=True)
            top = part if top is None else jnp.maximum(top, part)
        e_tiles = [jnp.exp2((s - top) * (scale * LOG2E)) for s in s_tiles]
        total = sum(jnp.sum(e, axis=0, keepdims=True) for e in e_tiles)
        inverse = 1.0 / total
        p_tiles = [e * inverse for e in e_tiles]
        probs.append(p_tiles)
        weight_cols.append(column([p.astype(jnp.bfloat16) for p in p_tiles], first, last))
    weights = jnp.concatenate(weight_cols, axis=1)
    attended_t = dot(values_t, weights).astype(jnp.bfloat16)
    delta = jnp.sum(attended_t.astype(jnp.float32) * douts_t.astype(jnp.float32), axis=0, keepdims=True)
    grad_cols = []
    for b, (first, last) in enumerate(columns):
        lanes = slice(b * tile, (b + 1) * tile)
        g_tiles = [
            (p * (dprobs[j * tile : (j + 1) * tile, lanes] - delta[:, lanes])).astype(jnp.bfloat16)
            for j, p in zip(range(first, last), probs[b])
        ]
        grad_cols.append(column(g_tiles, first, last))
    return weights, jnp.concatenate(grad_cols, axis=1), attended_t


def product_stage(weights, grads, attended_t, queries, douts, keys_t, scale):
    grad_q = (dot(keys_t, grads) * scale).astype(jnp.bfloat16).T
    return attended_t.T, grad_q, dot(grads, queries), dot(weights, douts)


def staged(blocks, scores_of, softmax_of, products_of, ahead=1):
    scores = {}
    for step in range(blocks + ahead):
        if step < blocks:
            scores[step] = scores_of(step)
        if step >= ahead:
            block = step - ahead
            products_of(block, *softmax_of(block, *scores.pop(block)))


def causal(s, tile):
    key = lax.broadcasted_iota(jnp.int32, (tile, tile), 0)
    query = lax.broadcasted_iota(jnp.int32, (tile, tile), 1)
    return jnp.where(key <= query, s, NEG)


def short_kernel(head, heads, lengths, dests, q_hbm, k_hbm, v_hbm, d_hbm, *rest):
    if head > 0:
        rest = rest[5:]
    else:
        order, rest = rest[0], rest[1:]
    out_hbm, dq_hbm, dk_hbm, dv_hbm = rest[:4]
    rest = rest[4:]
    if head == 0:
        (tail_ref, table_ref), rest = rest[:2], rest[2:]
        for index in range(order.shape[0]):
            table_ref[index : index + 1, :] = jnp.full((1, table_ref.shape[1]), order[index], jnp.int32)
    held, made, in_sem, out_sem = rest[:4]
    scale = HEAD_DIM ** (-0.5)
    tokens = q_hbm.shape[0]
    tile = tokens // 6
    span = 2 * tile
    rank = lax.axis_index("dp")
    count = lengths.shape[1]
    column = pl.ds(head * HEAD_DIM, HEAD_DIM)

    loads = [
        pltpu.make_async_copy(ref.at[:, column], held.at[slot], in_sem)
        for slot, ref in enumerate((q_hbm, k_hbm, v_hbm, d_hbm))
    ]
    for load in loads:
        load.start()
    others = []
    if head == 0:
        ends, end_sem = rest[4:]
        for other in range(1, heads):
            columns = pl.ds(other * HEAD_DIM, HEAD_DIM)
            for slot, ref in enumerate((q_hbm, k_hbm, v_hbm)):
                others.append(
                    pltpu.make_async_copy(
                        ref.at[pl.ds(tokens - 3 * tile, 3 * tile), columns],
                        ends.at[other - 1, slot],
                        end_sem,
                    )
                )
        for load in others:
            load.start()

    place = lax.broadcasted_iota(jnp.int32, (1, tokens), 1)
    start = jnp.zeros((1, tokens), jnp.int32)
    begin = jnp.int32(0)
    for j in range(count - 1):
        begin = begin + lengths[rank, j]
        start = jnp.where(place >= begin, begin, start)
    tail = lengths[rank, count - 1]
    moves = dests[rank, count - 1] != rank

    def store(slot, low, high, target):
        rows = pl.ds(low, high - low)
        pltpu.make_async_copy(made.at[slot, rows, :], target.at[rows, column], out_sem).start()

    pltpu.make_async_copy(held, held, in_sem).wait()
    q_ref, k_ref, v_ref, d_ref = [held.at[slot] for slot in range(4)]
    keys_t = k_ref[...].T
    values_t = v_ref[...].T
    douts_t = d_ref[...].T
    blocks = tokens // span
    pending = {}

    def key_low(block):
        return max(0, (block - 1) * span)

    def sent(last):
        to = lax.broadcasted_iota(jnp.int32, (tile, tile), 0)
        come = lax.broadcasted_iota(jnp.int32, (tile, tile), 1)
        pick = (come == to + (tile - tail)) & moves & (to < tail)
        return dot(pick.astype(jnp.float32).astype(jnp.bfloat16), last).astype(jnp.bfloat16)

    def scores_of(block):
        low = block * span
        keys = slice(key_low(block), low + span)
        return score_stage(q_ref[low : low + span, :], d_ref[low : low + span, :], k_ref[keys, :], v_ref[keys, :])

    def softmax_of(block, scores, dprobs):
        low = block * span
        offset = (low - key_low(block)) // tile

        def mask_tile(s, j, b):
            key = lax.broadcasted_iota(jnp.int32, (tile, tile), 0)
            first = start[:, low + b * tile : low + (b + 1) * tile] - (key_low(block) + j * tile)
            allowed = key >= first
            if j == offset + b:
                query = lax.broadcasted_iota(jnp.int32, (tile, tile), 1)
                allowed = allowed & (key <= query)
            return jnp.where(allowed, s, NEG)

        columns = [(max(0, offset + b - 2), offset + b + 1) for b in range(2)]
        keys = slice(key_low(block), low + span)
        return softmax_stage(
            scores, dprobs, values_t[:, keys], douts_t[:, low : low + span], tile, columns, mask_tile, scale
        )

    def products_of(block, weights, grads, attended_t):
        low = block * span
        high = low + span
        keys = slice(key_low(block), high)
        attended, grad_q, grad_k, grad_v = product_stage(
            weights,
            grads,
            attended_t,
            q_ref[low:high, :],
            d_ref[low:high, :],
            keys_t[:, keys],
            scale,
        )
        made[1, low:high, :] = grad_q
        store(1, low, high, dq_hbm)
        if high == tokens:
            last = attended[tile:, :]
            row = lax.broadcasted_iota(jnp.int32, (tile, 1), 0)
            kept = jnp.logical_not(moves & (row >= tile - tail))
            made[0, low : low + tile, :] = attended[:tile, :]
            made[0, low + tile : tokens, :] = jnp.where(kept, last, jnp.zeros_like(last))
            if head == 0:
                tail_ref[0] = sent(last)
        else:
            made[0, low:high, :] = attended
        store(0, low, high, out_hbm)
        if block > 0:
            done_k = pending["k"] + grad_k[:span]
            done_v = pending["v"] + grad_v[:span]
            made[2, low - span : low, :] = (done_k * scale).astype(jnp.bfloat16)
            made[3, low - span : low, :] = done_v.astype(jnp.bfloat16)
            store(2, low - span, low, dk_hbm)
            store(3, low - span, low, dv_hbm)
        pending["k"] = grad_k[-span:]
        pending["v"] = grad_v[-span:]
        if high == tokens:
            made[2, low:high, :] = (pending["k"] * scale).astype(jnp.bfloat16)
            made[3, low:high, :] = pending["v"].astype(jnp.bfloat16)
            store(2, low, high, dk_hbm)
            store(3, low, high, dv_hbm)

    staged(blocks, scores_of, softmax_of, products_of)
    if others:
        pltpu.make_async_copy(ends, ends, end_sem).wait()
        for other in range(1, heads):
            scores = dot_rows(ends[other - 1, 1], ends[other - 1, 0, 2 * tile :, :])
            key = lax.broadcasted_iota(jnp.int32, scores.shape, 0)
            query = lax.broadcasted_iota(jnp.int32, scores.shape, 1) + 2 * tile
            first = start[:, tokens - tile :] - (tokens - 3 * tile)
            scores = jnp.where((key >= first) & (key <= query), scores, NEG)
            grown = jnp.exp2((scores - jnp.max(scores, axis=0, keepdims=True)) * (scale * LOG2E))
            weights = (grown * (1.0 / jnp.sum(grown, axis=0, keepdims=True))).astype(jnp.bfloat16)
            tail_ref[other] = sent(dot(weights.T, ends[other - 1, 2]).astype(jnp.bfloat16))
    pltpu.make_async_copy(made, made, out_sem).wait()


def short_attention(head, heads, lengths, dests, arrays, before, after, order=None):
    tokens, width = arrays[0].shape
    move = tokens // 6
    smem = pl.BlockSpec(memory_space=pltpu.SMEM)
    hbm = pl.BlockSpec(memory_space=pltpu.HBM)
    vmem = pl.BlockSpec(memory_space=pltpu.VMEM)
    wide = jax.ShapeDtypeStruct((tokens, width), jnp.bfloat16)
    first = before is None
    extra = [order] if first else list(before[:4]) + [after]
    tile = move
    return pl.pallas_call(
        functools.partial(short_kernel, head, heads),
        in_specs=[smem] * 2 + [hbm] * 4 + ([smem] if first else [hbm] * 4 + [pl.BlockSpec(memory_space=pl.ANY)]),
        out_specs=[hbm] * 4 + ([vmem] * 2 if first else []),
        out_shape=[jax.ShapeDtypeStruct((tokens + move, width), jnp.bfloat16), wide, wide, wide]
        + (
            [
                jax.ShapeDtypeStruct((heads, move, HEAD_DIM), jnp.bfloat16),
                jax.ShapeDtypeStruct((order.shape[0], HEAD_DIM), jnp.int32),
            ]
            if first
            else []
        ),
        scratch_shapes=[
            pltpu.VMEM((4, tokens, HEAD_DIM), jnp.bfloat16),
            pltpu.VMEM((4, tokens, HEAD_DIM), jnp.bfloat16),
            pltpu.SemaphoreType.DMA,
            pltpu.SemaphoreType.DMA,
        ]
        + (
            [
                pltpu.VMEM((max(heads - 1, 1), 3, 3 * tile, HEAD_DIM), jnp.bfloat16),
                pltpu.SemaphoreType.DMA,
            ]
            if first
            else []
        ),
        input_output_aliases={} if first else {6 + i: i for i in range(4)},
        compiler_params=pltpu.CompilerParams(vmem_limit_bytes=16 << 20),
        cost_estimate=pl.CostEstimate(flops=10**9, bytes_accessed=3 * 10**6, transcendentals=0),
    )(lengths, dests, *arrays, *extra)


def peer_order(ways):
    return [step for step in range(2, ways)] + [1]


def pack_kernel(parts, ways, after, q_ref, k_ref, v_ref, d_ref, *rest):
    rest = rest[after:]
    outs, (all_bytes, sem) = rest[: len(parts)], rest[len(parts) :]
    own = lax.axis_index("ctx")
    per = q_ref.shape[2] // ways
    for out, (head, step) in zip(outs, parts):
        column = pl.multiple_of((own ^ step) * per + head * HEAD_DIM, HEAD_DIM)
        for slot, ref in enumerate((q_ref, k_ref, v_ref, d_ref)):
            pltpu.make_async_copy(ref.at[0, :, pl.ds(column, HEAD_DIM)], out.at[slot], sem).start()
    pltpu.make_async_copy(all_bytes, all_bytes, sem).wait()


def pack(parts, ways, arrays, after=()):
    rows = arrays[0].shape[1]
    return pl.pallas_call(
        functools.partial(pack_kernel, parts, ways, len(after)),
        in_specs=[pl.BlockSpec(memory_space=pl.ANY if after else pltpu.HBM)] * 4
        + [pl.BlockSpec(memory_space=pl.ANY)] * len(after),
        out_specs=[pl.BlockSpec(memory_space=pltpu.VMEM)] * len(parts),
        out_shape=[jax.ShapeDtypeStruct((4, rows, HEAD_DIM), jnp.bfloat16)] * len(parts),
        scratch_shapes=[
            pltpu.VMEM((4 * len(parts), rows, HEAD_DIM), jnp.bfloat16),
            pltpu.SemaphoreType.DMA,
        ],
        compiler_params=pltpu.CompilerParams(vmem_limit_bytes=8 << 20),
        cost_estimate=pl.CostEstimate(flops=0, bytes_accessed=2 * 10**6, transcendentals=0),
    )(*[array if after else pltpu.with_memory_space_constraint(array, pltpu.HBM) for array in arrays], *after)


def long_kernel(ways, linked, order, *rest):
    rest = rest[linked:]
    steps = peer_order(ways) + [0]
    arrived = rest[:ways]
    outs = rest[ways : 2 * ways]
    held, made = rest[2 * ways :]
    scale = HEAD_DIM ** (-0.5)
    own = lax.axis_index("ctx")
    rows = arrived[0].shape[1]
    half = rows // 2
    total = rows * ways

    def spot(device, part):
        return pl.ds(pl.multiple_of(order[device * 2 + part, 0] * half, half), half)

    for buffer, step in zip(arrived, steps):
        for part in range(2):
            piece = slice(part * half, (part + 1) * half)
            for slot in range(4):
                held[slot, spot(own ^ step, part), :] = buffer[slot, piece, :]

    tile = HEAD_DIM
    span = 2 * tile
    blocks = total // span
    keys_t = held[1].T
    values_t = held[2].T
    douts_t = held[3].T
    sum_k = [None] * blocks
    sum_v = [None] * blocks

    def scores_of(block):
        low, high = block * span, (block + 1) * span
        return score_stage(held[0, low:high, :], held[3, low:high, :], held[1, :high, :], held[2, :high, :])

    def softmax_of(block, scores, dprobs):
        first = block * span // tile

        def mask_tile(s, j, b):
            return causal(s, tile) if j == first + b else s

        columns = [(0, first + b + 1) for b in range(span // tile)]
        low, high = block * span, (block + 1) * span
        return softmax_stage(
            scores, dprobs, values_t[:, :high], douts_t[:, low:high], tile, columns, mask_tile, scale
        )

    def products_of(block, weights, grads, attended_t):
        low, high = block * span, (block + 1) * span
        attended, grad_q, grad_k, grad_v = product_stage(
            weights, grads, attended_t, held[0, low:high, :], held[3, low:high, :], keys_t[:, :high], scale
        )
        made[0, low:high, :] = attended
        made[1, low:high, :] = grad_q
        for part in range(block + 1):
            piece = slice(part * span, (part + 1) * span)
            sum_k[part] = grad_k[piece] if sum_k[part] is None else sum_k[part] + grad_k[piece]
            sum_v[part] = grad_v[piece] if sum_v[part] is None else sum_v[part] + grad_v[piece]

    staged(blocks, scores_of, softmax_of, products_of)
    for part in range(blocks):
        piece = slice(part * span, (part + 1) * span)
        made[2, piece, :] = (sum_k[part] * scale).astype(jnp.bfloat16)
        made[3, piece, :] = sum_v[part].astype(jnp.bfloat16)

    for out, step in zip(outs, steps):
        for part in range(2):
            piece = slice(part * half, (part + 1) * half)
            for slot in range(4):
                out[slot, piece, :] = made[slot, spot(own ^ step, part), :]


def long_attention(ways, order, arrived, linked=()):
    anywhere = [pl.BlockSpec(memory_space=pl.ANY)] * len(linked)
    rows = arrived[0].shape[1]
    piece = jax.ShapeDtypeStruct((4, rows, HEAD_DIM), jnp.bfloat16)
    vmem = pl.BlockSpec(memory_space=pltpu.VMEM)
    return pl.pallas_call(
        functools.partial(long_kernel, ways, len(linked)),
        in_specs=[vmem] + anywhere + [vmem] * ways,
        out_specs=[vmem] * ways,
        out_shape=[piece] * ways,
        scratch_shapes=[
            pltpu.VMEM((4, rows * ways, HEAD_DIM), jnp.bfloat16),
            pltpu.VMEM((4, rows * ways, HEAD_DIM), jnp.bfloat16),
        ],
        compiler_params=pltpu.CompilerParams(vmem_limit_bytes=16 << 20),
        cost_estimate=pl.CostEstimate(flops=10**9, bytes_accessed=3 * 10**6, transcendentals=0),
    )(order, *linked, *arrived)


def join_kernel(parts, ways, olds, with_short, *refs):
    pieces = refs[: len(parts)]
    refs = refs[len(parts) :]
    if with_short:
        received, refs = refs[0], refs[1:]
    refs = refs[olds:]
    outs, refs = refs[:4], refs[4:]
    all_bytes, sem = refs[-2:]
    own = lax.axis_index("ctx")
    per = outs[0].shape[2] // ways
    for piece, (head, step) in zip(pieces, parts):
        column = pl.multiple_of((own ^ step) * per + head * HEAD_DIM, HEAD_DIM)
        for slot, out in enumerate(outs):
            pltpu.make_async_copy(piece.at[slot], out.at[0, :, pl.ds(column, HEAD_DIM)], sem).start()
    if with_short:
        short_out = refs[0]
        heads, move, _ = received.shape
        rows = pl.ds(short_out.shape[0] - move, move)
        for other in range(heads):
            columns = pl.ds(other * HEAD_DIM, HEAD_DIM)
            pltpu.make_async_copy(received.at[other], short_out.at[rows, columns], sem).start()
    pltpu.make_async_copy(all_bytes, all_bytes, sem).wait()


def join(parts, ways, pieces, outs, shape, received=None, short_out=None):
    with_short = received is not None
    vmem = pl.BlockSpec(memory_space=pltpu.VMEM)
    hbm = pl.BlockSpec(memory_space=pltpu.HBM)
    operands = list(pieces)
    in_specs = [vmem] * len(pieces)
    out_shape = [jax.ShapeDtypeStruct(shape, jnp.bfloat16)] * 4
    aliases = {}
    size = 4 * len(parts) * shape[1]
    if with_short:
        operands.append(received)
        in_specs.append(vmem)
        out_shape.append(jax.ShapeDtypeStruct(short_out.shape, jnp.bfloat16))
        size += received.shape[0] * received.shape[1]
    old = ([] if outs is None else list(outs)) + ([short_out] if with_short else [])
    first_out = 0 if outs is not None else 4
    for index, value in enumerate(old):
        aliases[len(operands)] = first_out + index
        operands.append(value)
        in_specs.append(hbm)
    return pl.pallas_call(
        functools.partial(join_kernel, parts, ways, len(old), with_short),
        in_specs=in_specs,
        out_specs=[hbm] * len(out_shape),
        out_shape=out_shape,
        scratch_shapes=[pltpu.VMEM((size, HEAD_DIM), jnp.bfloat16), pltpu.SemaphoreType.DMA],
        input_output_aliases=aliases,
        compiler_params=pltpu.CompilerParams(vmem_limit_bytes=8 << 20),
        cost_estimate=pl.CostEstimate(flops=0, bytes_accessed=10**6, transcendentals=0),
    )(*operands)


def shards(
    q_short,
    k_short,
    v_short,
    dout_short,
    doc_lengths,
    doc_dest,
    q_long,
    k_long,
    v_long,
    dout_long,
    block_order,
):
    ways = lax.axis_size("ctx")
    ranks = lax.axis_size("dp")
    steps = peer_order(ways)
    heads_each = q_long.shape[2] // HEAD_DIM // ways
    arrays = (q_long, k_long, v_long, dout_long)

    def swap(value, step):
        return lax.ppermute(value, "ctx", [(i, i ^ step) for i in range(ways)])

    far = [step for step in steps if step != 1]
    first = [(0, step) for step in far]
    later = [(0, 1), (0, 0)] + [(head, step) for head in range(1, heads_each) for step in steps + [0]]
    packed = dict(zip(first, pack(first, ways, arrays)))
    packed.update(zip(later, pack(later, ways, arrays, (packed[first[0]],))))
    arrived = [[swap(packed[head, step], step) for step in steps] + [packed[head, 0]] for head in range(heads_each)]
    shorts = (q_short, k_short, v_short, dout_short)
    short_heads = q_short.shape[1] // HEAD_DIM
    short = short_attention(0, short_heads, doc_lengths, doc_dest, shorts, None, None, block_order)
    (tail, table), short = short[4:], short[:4]
    received = lax.ppermute(tail, "dp", [(i, (i + ranks // 2) % ranks) for i in range(ranks)])
    pieces = []
    for head in range(heads_each):
        made = long_attention(ways, table, arrived[head], (pieces[-1][-1] if head else tail,))
        pieces.append([swap(value, step) for value, step in zip(made[: ways - 1], steps)] + [made[-1]])
    for head in range(1, short_heads):
        short = short_attention(head, short_heads, doc_lengths, doc_dest, shorts, short, pieces[-1][-1])
    whole = {(head, step): pieces[head][index] for head in range(heads_each) for index, step in enumerate(steps + [0])}
    final = [(heads_each - 1, step) for step in far]
    sooner = [key for key in whole if key not in final]
    outs = join(sooner, ways, [whole[key] for key in sooner], None, q_long.shape)
    outs = join(final, ways, [whole[key] for key in final], outs[:4], q_long.shape, received, short[0])
    out_long, dq_long, dk_long, dv_long, out_short = outs
    dq_short, dk_short, dv_short = short[1:]
    return (out_short, dq_short, dk_short, dv_short, out_long, dq_long, dk_long, dv_long)


def solution(mesh):
    flat = P("dp", "ctx")
    deep = P("dp", "ctx", None)

    return jax.shard_map(
        shards,
        mesh=mesh,
        in_specs=(flat,) * 4 + (P(), P()) + (deep,) * 4 + (P(),),
        out_specs=(flat,) * 4 + (deep,) * 4,
        check_vma=False,
    )
```
